32 devices in a mesh: groups: 2 (over x), seq: 16 (over z, y, core).
Axes of the slice: x: 2, y: 2, z: 4, core: 2. Of those that a mesh axis runs over, the one named last changes fastest.
Arguments:
- prefill_q: bfloat16 [32, 8192], P(('groups', 'seq')), parts along dimension 0, may hold values from -48 to 48
- cache_k: bfloat16 [16384, 1024], P(('groups', 'seq')), parts along dimension 0, may hold values from -4.5 to 4.5
- cache_v: bfloat16 [16384, 1024], P(('groups', 'seq')), parts along dimension 0, may hold values from -4.5 to 4.5
- page_counts: int32 [32], P('groups'), parts along dimension 0, may hold values from 1 to 64, 768 in all
- page_owner: int32 [2048, 1], P(('groups', 'seq')), parts along dimension 0, may hold values from 0 to 15; in each aligned block of 64 rows (0 to 63, 64 to 127, ...) at most 8 rows name the same one
- decode_q: bfloat16 [32, 2, 8192], P(('groups', 'seq')), parts along dimension 0, may hold values from -48 to 48
- decode_k: bfloat16 [32, 2, 1024], P(('groups', 'seq')), parts along dimension 0, may hold values from -12 to 12
- decode_v: bfloat16 [32, 2, 1024], P(('groups', 'seq')), parts along dimension 0, may hold values from -4.5 to 4.5
- context_len: int32 [32], P(('groups', 'seq')), parts along dimension 0, may hold values from 768 to 6144
Outputs:
- prefill_out: bfloat16 [32, 8192], P(('groups', 'seq')), parts along dimension 0
- decode_out: bfloat16 [32, 2, 8192], P(('groups', 'seq')), parts along dimension 0
- store_k: bfloat16 [32768, 1024], P(('groups', 'seq')), parts along dimension 0
- store_v: bfloat16 [32768, 1024], P(('groups', 'seq')), parts along dimension 0
- store_page: int32 [4096], P(('groups', 'seq')), parts along dimension 0
The draws below stay inside these ranges and needn't reach their ends.
There are 2 independent parts, one for each index of `groups`. The reference program is written for one: setup_inputs(seed, part) draws one part's arguments, and reference() takes and returns one part's arrays. A program takes and returns all parts, laid end to end along the dimension named above; each array names one. Nothing has to cross between parts.
Inputs may be any that keep to these rules, and one draw needn't show every extreme that they name: `page_counts`: the counts sum to 768 and the largest equals 64. `page_owner`: within the 64 page slots of one shard each owner is named at most 8 times, and exactly 8 times in some shards.
All inputs are finite; a program needn't handle non-finite values.
Results may differ from the reference program's by a relative error of at most 0.014.
Values may be sent and summed in bfloat16 or wider, within the bound.
A program may use at most 128 MiB of HBM per device.

```python
import math
import jax
import jax.numpy as jnp
import numpy as np
from jax import lax

HQ = 64
KVH = 8
HD = 128
PAGE = 8
PPD = 64
STEPS = 2
KVD = 1024
CAP = 8
TOTAL_PAGES = 768
SLOTS = 1024
STORE = 2048
SPAN = 16
REQ = 16
N_SEQ = 16


def shared_keys(key):
    base_key = jax.random.fold_in(key, 11)
    key_table = jnp.clip(jax.random.normal(base_key, (SLOTS * PAGE, KVD), jnp.float32), -4.5, 4.5)
    return key_table


def shared_queries(key, height, salt_value):
    base_key = jax.random.fold_in(key, salt_value)
    drawn_rows = jnp.clip(2.5 * jax.random.normal(base_key, (height, HQ * HD), jnp.float32), -15.0, 15.0)
    final_rows = drawn_rows
    return (drawn_rows, final_rows)


def draw_prefill_q(key, part):
    return shared_queries(key, SPAN, 31)[1].astype(jnp.bfloat16)


def draw_cache_k(key, part):
    return shared_keys(key).astype(jnp.bfloat16)


def draw_decode_q(key, part):
    return shared_queries(key, REQ * STEPS, 41)[1].reshape(REQ, STEPS, HQ * HD).astype(jnp.bfloat16)


def draw_decode_k(key, part):
    drawn_rows = shared_queries(key, REQ * STEPS, 41)[0]
    grouping = HQ // KVH
    summed = jnp.sum(drawn_rows.reshape(REQ * STEPS, KVH, grouping, HD), axis=2) * (0.5 / jnp.sqrt(jnp.float32(grouping)))
    noise_part = 0.5 * jax.random.normal(jax.random.fold_in(key, 51), (REQ * STEPS, KVH, HD), jnp.float32)
    return jnp.clip(summed + noise_part, -12.0, 12.0).reshape(REQ, STEPS, KVH * HD).astype(jnp.bfloat16)


def with_ends(values, key, smallest, largest):
    longest = values.shape.index(max(values.shape))
    spots = []
    for shift in (0, 1):
        where = [jax.random.randint(jax.random.fold_in(key, axis), (), 0, length) for axis, length in enumerate(values.shape)]
        where[longest] = (where[longest] + shift) % values.shape[longest]
        spots.append(tuple(where))
    return values.at[spots[0]].set(smallest).at[spots[1]].set(largest)


def level_of(stream_key, shape, pieces, least, largest):
    gain, own = 1.0, jax.random.fold_in(stream_key, 6)
    for dim, shards_of in pieces:
        heights = jnp.exp(jax.random.uniform(jax.random.fold_in(own, dim), (shards_of,), jnp.float32, least / len(pieces), largest / len(pieces)))
        gain = gain * jnp.repeat(heights, shape[dim] // shards_of).reshape([-1 if axis == dim else 1 for axis in range(len(shape))])
    return gain


def length_profile(amount, total, most, skew):
    portions = [(1 << 20) // math.isqrt(grade ** skew) + 1 for grade in range(2, amount + 1)]
    spare, holding = total - most - (amount - 1), [1] * (amount - 1)
    while spare > 0:
        movable = [i for i in range(amount - 1) if holding[i] < most]
        pool, remaining = sum([portions[i] for i in movable]), spare
        for i in movable:
            extra = min(most - holding[i], max(1, remaining * portions[i] // pool), spare)
            holding[i] = holding[i] + extra
            spare = spare - extra
    return np.array([most] + holding)


def ragged_sizes(rng, number_of, total, most, skew):
    if number_of == 2:
        one = jax.random.randint(rng, (), max(1, total - most), min(most, total - 1) + 1)
        return jnp.stack([one, total - one])
    lengths = jnp.asarray(length_profile(number_of, total, most, skew), jnp.int32)
    pairs = (number_of - 1) // 2
    giver, taker = lengths[1:1 + 2 * pairs:2], lengths[2:2 + 2 * pairs:2]
    slack = jnp.minimum(giver - 1, most - taker)
    moved = jax.random.randint(jax.random.fold_in(rng, 1), (pairs,), 0, 1 << 20) % (slack + 1)
    lengths = lengths.at[1:1 + 2 * pairs:2].set(giver - moved).at[2:2 + 2 * pairs:2].set(taker + moved)
    return lengths[jax.random.permutation(jax.random.fold_in(rng, 2), number_of)]


def shared_out(own_key, own, number, rows, number_of, top, bound, lean):
    order = jax.random.permutation(own_key, number_of)
    packed, usual = load_shares(number_of, rows * top, bound, lean, True), load_shares(number_of, rows * top, bound, lean, False)
    places = jnp.arange(number_of)

    def named(tallies, rotation):
        used = int((tallies > 0).sum())
        fixed = max(1, used // 4)
        moved = fixed + (places - fixed + rotation * (used - fixed)) % max(1, number_of - fixed)
        return jnp.zeros((number_of,), jnp.int32).at[order[jnp.where(places < fixed, places, moved)]].set(jnp.asarray(tallies, jnp.int32))

    tallies = jnp.where(number % 4 == 0, named(packed, number // 4), named(usual, number - number // 4 - 1))
    mixed = jax.random.permutation(jax.random.fold_in(own, 3), number_of)
    source_of, taker = mixed[0:number_of // 2 * 2:2], mixed[1:number_of // 2 * 2:2]
    room = jnp.minimum(tallies[source_of] - 1, bound - tallies[taker]) // 2
    room = jnp.where((source_of == order[0]) | (taker == order[0]) | (tallies[taker] == 0), 0, jnp.maximum(room, 0))
    moved = jax.random.randint(jax.random.fold_in(own, 4), (number_of // 2,), 0, 1 << 20) % (room + 1)
    tallies = tallies.at[source_of].add(-moved).at[taker].add(moved)
    members = jnp.searchsorted(jnp.cumsum(tallies), jnp.arange(rows * top), side="right").astype(jnp.int32)
    table = members.reshape(top, rows).T
    table = table[jax.random.permutation(jax.random.fold_in(own, 1), rows)]
    rotation = jax.random.randint(jax.random.fold_in(own, 2), (rows, 1), 0, top)
    return jnp.take_along_axis(table, (jnp.arange(top)[None, :] + rotation) % top, axis=1)


def load_shares(number_of, total, most, slope, full):
    portions = [(1 << 20) // math.isqrt(standing ** slope) + 1 for standing in range(1, number_of + 1)]
    largest = most if full else min(most, max(-(-total // number_of), total * portions[0] // sum(portions)))
    least = 1 if total - largest >= number_of - 1 else 0
    given, rest = [largest] + [least] * (number_of - 1), total - largest - least * (number_of - 1)
    while rest > 0:
        candidates = [i for i in range(1, number_of) if given[i] < largest] or [i for i in range(1, number_of) if given[i] < most]
        mass, left = sum([portions[i] for i in candidates]), rest
        for i in candidates:
            addition = min(most - given[i], max(1, left * portions[i] // mass), rest)
            given[i] = given[i] + addition
            rest = rest - addition
    return np.array(given)


def bell_draw(own_key, dims, spread, limit, shards=(), held_as=jnp.bfloat16):
    drawn = spread * jax.random.normal(own_key, dims, jnp.float32)
    if shards:
        drawn = drawn * level_of(own_key, dims, shards, -0.22, 0.18)
    return jnp.clip(drawn, -limit, limit).astype(held_as)


def setup_inputs(seed: int = 0, part: int = 0) -> dict:
    splits = jax.random.split(jax.random.key(seed), 10)
    part_keys = jax.random.split(jax.random.fold_in(splits[9], part), 10)
    prefill_q = draw_prefill_q(jax.random.fold_in(jax.random.fold_in(splits[9], part), 71), part)
    cache_k = draw_cache_k(jax.random.fold_in(jax.random.fold_in(splits[9], part), 71), part)
    cache_v = bell_draw(part_keys[2], (SLOTS * PAGE, KVD), 1.0, 4.5, ((0, 16),))
    page_counts = ragged_sizes(part_keys[3], N_SEQ, TOTAL_PAGES, PPD, 2).astype(jnp.int32)
    page_owner_keys = jax.random.split(jax.random.fold_in(part_keys[4], 1), SLOTS // PPD)
    page_owner_turns = jax.random.permutation(jax.random.fold_in(part_keys[4], 3), SLOTS // PPD)
    page_owner = jax.vmap(lambda own, number: shared_out(jax.random.fold_in(part_keys[4], 2), own, number, PPD, N_SEQ, 1, CAP, 2))(page_owner_keys, page_owner_turns).reshape((SLOTS, 1))
    decode_q = draw_decode_q(jax.random.fold_in(jax.random.fold_in(splits[9], part), 71), part)
    decode_k = draw_decode_k(jax.random.fold_in(jax.random.fold_in(splits[9], part), 71), part)
    decode_v = bell_draw(part_keys[7], (REQ, STEPS, KVD), 1.0, 4.5, ((0, 16),))
    context_len = with_ends(jax.random.randint(part_keys[8], (REQ,), PAGE * TOTAL_PAGES // 8, PAGE * TOTAL_PAGES + 1), jax.random.fold_in(part_keys[8], 1), PAGE * TOTAL_PAGES // 8, PAGE * TOTAL_PAGES).astype(jnp.int32)
    return dict(prefill_q=prefill_q, cache_k=cache_k, cache_v=cache_v, page_counts=page_counts, page_owner=page_owner, decode_q=decode_q, decode_k=decode_k, decode_v=decode_v, context_len=context_len)


MASKED = -1.0e30
EXACT = lax.Precision.HIGHEST


def attention(queries, key_block, value_block, allowed, own_keys, own_values, own_allowed):
    height = queries.shape[0]
    grouping = HQ // KVH
    scaling = HD ** -0.5
    query_all = queries.astype(jnp.float32).reshape(height, KVH, grouping, HD)
    key_all = key_block.astype(jnp.float32).reshape(-1, KVH, HD)
    value_all = value_block.astype(jnp.float32).reshape(-1, KVH, HD)
    if own_keys is not None:
        own_key_all = own_keys.astype(jnp.float32).reshape(height, -1, KVH, HD)
        own_value_all = own_values.astype(jnp.float32).reshape(height, -1, KVH, HD)

    def per_group(member):
        query_group = lax.dynamic_index_in_dim(query_all, member, 1, keepdims=False)
        key_group = lax.dynamic_index_in_dim(key_all, member, 1, keepdims=False)
        value_group = lax.dynamic_index_in_dim(value_all, member, 1, keepdims=False)
        scores = jnp.einsum("qhd,kd->qhk", query_group, key_group, precision=EXACT) * scaling
        scores = jnp.where(allowed[:, None, :], scores, MASKED)
        highest = jnp.max(scores, axis=2)
        if own_keys is not None:
            own_key_group = lax.dynamic_index_in_dim(own_key_all, member, 2, keepdims=False)
            own_value_group = lax.dynamic_index_in_dim(own_value_all, member, 2, keepdims=False)
            own_scores = jnp.einsum("qhd,qtd->qht", query_group, own_key_group, precision=EXACT) * scaling
            own_scores = jnp.where(own_allowed[:, None, :], own_scores, MASKED)
            highest = jnp.maximum(highest, jnp.max(own_scores, axis=2))
        weights = jnp.where(allowed[:, None, :], jnp.exp(scores - highest[:, :, None]), 0.0)
        totals = jnp.sum(weights, axis=2)
        if own_keys is not None:
            own_weights = jnp.where(own_allowed[:, None, :], jnp.exp(own_scores - highest[:, :, None]), 0.0)
            totals = totals + jnp.sum(own_weights, axis=2)
        probs = lax.optimization_barrier((weights / totals[:, :, None]).astype(jnp.bfloat16)).astype(jnp.float32)
        result = jnp.einsum("qhk,kd->qhd", probs, value_group, precision=EXACT)
        if own_keys is not None:
            own_probs = lax.optimization_barrier((own_weights / totals[:, :, None]).astype(jnp.bfloat16)).astype(jnp.float32)
            result = result + jnp.einsum("qht,qtd->qhd", own_probs, own_value_group, precision=EXACT)
        return result

    outputs = lax.map(per_group, jnp.arange(KVH, dtype=jnp.int32))
    return outputs.transpose(1, 0, 2, 3).reshape(height, HQ * HD).astype(jnp.bfloat16)


def reference(prefill_q, cache_k, cache_v, page_counts, page_owner, decode_q, decode_k, decode_v, context_len):
    shard_rows = PPD * PAGE
    key_rows = jnp.arange(SLOTS * PAGE, dtype=jnp.int32)
    device_of = key_rows // shard_rows
    local_row = key_rows % shard_rows
    before = (jnp.cumsum(page_counts) - page_counts).astype(jnp.int32)
    usable = local_row < PAGE * page_counts[device_of]
    places = PAGE * before[device_of] + local_row
    prompt = PAGE * jnp.sum(page_counts).astype(jnp.int32)
    query_places = prompt - SPAN + jnp.arange(SPAN, dtype=jnp.int32)
    allowed = usable[None, :] & (places[None, :] <= query_places[:, None])
    prefill_out = attention(prefill_q, cache_k, cache_v, allowed, None, None, None)

    query_rows = decode_q.reshape(REQ * STEPS, HQ * HD)
    limits = jnp.repeat(context_len, STEPS)
    decode_allowed = usable[None, :] & (places[None, :] < limits[:, None])
    own_keys = jnp.repeat(decode_k, STEPS, axis=0)
    own_values = jnp.repeat(decode_v, STEPS, axis=0)
    steps_now = jnp.tile(jnp.arange(STEPS, dtype=jnp.int32), REQ)
    own_allowed = jnp.arange(STEPS, dtype=jnp.int32)[None, :] <= steps_now[:, None]
    decode_out = attention(query_rows, cache_k, cache_v, decode_allowed, own_keys, own_values, own_allowed)
    decode_out = decode_out.reshape(REQ, STEPS, HQ * HD)

    owners = page_owner[:, 0]
    page_index = jnp.arange(SLOTS, dtype=jnp.int32)
    page_device = page_index // PPD
    page_live = (page_index % PPD) < page_counts[page_device]
    chosen = owners[:, None] == jnp.arange(N_SEQ, dtype=jnp.int32)[None, :]
    chosen_live = (chosen & page_live[:, None]).astype(jnp.int32).reshape(N_SEQ, PPD, N_SEQ)
    earlier = (jnp.cumsum(chosen_live, axis=1) - chosen_live).astype(jnp.int32).reshape(SLOTS, N_SEQ)
    ranking = jnp.sum(earlier * chosen.astype(jnp.int32), axis=1).astype(jnp.int32)
    target = jnp.where(page_live, owners * (N_SEQ * CAP) + page_device * CAP + ranking, STORE).astype(jnp.int32)
    store_k = jnp.zeros((STORE, PAGE * KVD), cache_k.dtype).at[target].set(cache_k.reshape(SLOTS, PAGE * KVD), mode="drop")
    store_v = jnp.zeros((STORE, PAGE * KVD), cache_v.dtype).at[target].set(cache_v.reshape(SLOTS, PAGE * KVD), mode="drop")
    store_page = jnp.full((STORE,), -1, jnp.int32).at[target].set(page_index, mode="drop")
    return prefill_out, decode_out, store_k.reshape(STORE * PAGE, KVD), store_v.reshape(STORE * PAGE, KVD), store_page
```

```python
import functools

import jax
import jax.numpy as jnp
from jax import lax
from jax.experimental import pallas as pl
from jax.experimental.pallas import tpu as pltpu
from jax.sharding import PartitionSpec as P

HQ = 64
KVH = 8
HD = 128
PAGE = 8
STEPS = 2
KVD = 1024
GROUP = HQ // KVH
ROWS = (1 + STEPS) * GROUP
LANES = 128
MASKED = -1e30
SCALE = HD ** (-0.5)
MESH = pl.DeviceIdType.MESH

META, KEYS, VALUES = range(3)
QROW, PART, STAT = range(3)
IDS, ROUTE = range(2)


def plan(n, cap):
    if n // 4 != 4 or n % 4:
        return False, 0, 0
    most = cap * n // 2
    return True, most * 11 // 16, most // 2 * 7 // 8


def pieces_of(parts):
    width = KVD // parts
    return [(kind, i * width, width) for kind in (KEYS, VALUES) for i in range(parts)]


def prep_kernel(
    n, cap, page_slots, split, dense, tail,
    owner, counts, context, ck_hbm, cv_hbm, pq, dq,
    out_k, out_v, *rest,
):
    if split:
        cross_k, cross_v, q_out, meta, ck, cv, table, seen, cross, tally, done = rest
    else:
        q_out, meta, ck, cv, table, seen, done = rest
    me = lax.axis_index("seq")
    my_z, plane = me // 4, me % 4
    half = my_z // 2
    span = n // 2 if split else n
    base = half * span if split else 0
    loads = [
        pltpu.make_async_copy(ck_hbm, ck, done.at[0]),
        pltpu.make_async_copy(cv_hbm, cv, done.at[1]),
    ]
    for load in loads:
        load.start()

    for s in range(1 + STEPS):
        for h in range(HQ):
            row = s * GROUP + h % GROUP
            src = pq if s == 0 else dq
            at = 0 if s == 0 else s - 1
            q_out[h // GROUP, row : row + 1, :] = src[at : at + 1, h * HD : (h + 1) * HD]

    def clear(i, _):
        seen[i] = 0
        for k in range(cap):
            table[i * cap + k] = -1
            meta[i, IDS, me * cap + k] = -1
        meta[i, ROUTE, 4 * cap] = context[0]
        return 0

    lax.fori_loop(0, n, clear, 0)
    if split:
        near = (2 - half) * 4 + plane
        far = 3 * (1 - half) * 4 + plane
        for k in range(4 * cap):
            meta[near, ROUTE, k] = -1
            meta[far, ROUTE, k] = -1

        def zero(i, _):
            cross[i] = 0
            return 0

        lax.fori_loop(0, dense, zero, 0)
        tally[0] = 0
        tally[1] = 0
        tally[2] = 0

    def place(j, _):
        o = owner[j]
        k = seen[o]
        seen[o] = k + 1
        table[o * cap + k] = j
        meta[o, IDS, me * cap + k] = me * page_slots + j
        if split:
            @pl.when(o // 4 // 2 != half)
            def _():
                front, back = tally[0], tally[1]
                room = front + back < dense
                at = (o % 4) * cap + k

                @pl.when(room & (o // 4 == 2 - half))
                def _():
                    cross[front] = j
                    meta[near, ROUTE, at] = front
                    tally[0] = front + 1

                fits = room & (back < tail)

                @pl.when(fits & (o // 4 != 2 - half))
                def _():
                    cross[dense - 1 - back] = j
                    meta[far, ROUTE, at] = tail - 1 - back
                    tally[1] = back + 1

                @pl.when(jnp.logical_not(jnp.where(o // 4 == 2 - half, room, fits)))
                def _():
                    tally[2] = 1

        return 0

    lax.fori_loop(0, counts[me], place, 0)

    if split:
        def flag(i, _):
            meta[i, ROUTE, 4 * cap + 1] = tally[2]
            return 0

        lax.fori_loop(0, n, flag, 0)

    for load in loads:
        load.wait()

    if split:
        def pick(i, _):
            page = cross[i]
            cross_k[i] = ck[page]
            cross_v[i] = cv[page]
            return 0

        lax.fori_loop(0, dense, pick, 0)

    def fill(i, _):
        for k in range(cap):
            src = table[(base + i) * cap + k]
            page = jnp.maximum(src, 0)
            there = jnp.full((PAGE, KVD), src, jnp.int32) >= 0
            out_k[i * cap + k] = jnp.where(there, ck[page], jnp.zeros((), out_k.dtype))
            out_v[i * cap + k] = jnp.where(there, cv[page], jnp.zeros((), out_v.dtype))
        return 0

    lax.fori_loop(0, span, fill, 0)


def prep(n, cap, split, owner, counts, context, ck, cv, pq, dq):
    page_slots = ck.shape[0]
    _, dense, tail = plan(n, cap)
    smem = pl.BlockSpec(memory_space=pltpu.SMEM)
    vmem = pl.BlockSpec(memory_space=pltpu.VMEM)
    hbm = pl.BlockSpec(memory_space=pltpu.HBM)
    span = n // 2 if split else n

    def pages(count):
        return [jax.ShapeDtypeStruct((count, PAGE, KVD), x.dtype) for x in (ck, cv)]

    out_shape = pages(span * cap) + (pages(dense) if split else [])
    out_specs = [vmem] * len(out_shape) + [vmem, smem]
    out_shape += [
        jax.ShapeDtypeStruct((KVH, ROWS, HD), pq.dtype),
        jax.ShapeDtypeStruct((n, 2, n * cap), jnp.int32),
    ]
    scratch = [
        pltpu.VMEM(ck.shape, ck.dtype), pltpu.VMEM(cv.shape, cv.dtype),
        pltpu.SMEM((n * cap,), jnp.int32), pltpu.SMEM((n,), jnp.int32),
    ]
    if split:
        scratch += [pltpu.SMEM((dense,), jnp.int32), pltpu.SMEM((4,), jnp.int32)]
    return pl.pallas_call(
        functools.partial(prep_kernel, n, cap, page_slots, split, dense, tail),
        in_specs=[smem, smem, smem, hbm, hbm, vmem, vmem],
        out_specs=out_specs,
        out_shape=out_shape,
        scratch_shapes=scratch + [pltpu.SemaphoreType.DMA((2,))],
        compiler_params=pltpu.CompilerParams(vmem_limit_bytes=16 << 20),
        name="prep",
    )(owner, counts, context, ck, cv, pq, dq)


def main_kernel(
    n, cap, chunk, split, dense, tail, parts,
    counts, q_ref, meta_ref, ck_hbm, cv_hbm, pk_ref, pv_ref, ok_ref, ov_ref, *rest,
):
    if split:
        mk_ref, mv_ref = rest[:2]
        rest = rest[2:]
    pre_out, dec_out, store_k, store_v, meta_out = rest[:5]
    rest = rest[5:]
    if split:
        flag_out = rest[0]
        rest = rest[1:]
    (
        ck_ref, cv_ref, meta_s,
        qbuf, obuf, stat, limit, got1, got1s, obuf1, stat1, got2, got2s, obuf2, stat2, pbuf, sbuf,
        page_send, page_recv, row_send, row_recv, pair_send, pair_recv, local,
    ) = rest[:24]
    rest = rest[24:]
    if split:
        (
            meta_x, meta_xs, *lands, fan_k, fan_v,
            x_send, x_recv, cross_send, cross_recv, pass_send, pass_recv, fan_send, fan_recv,
        ) = rest
    depth = n // 4
    groups = lax.axis_size("groups")
    my_g = lax.axis_index("groups")
    me = lax.axis_index("seq")
    my_z, my_y, my_c = me // 4, (me // 2) % 2, me % 2
    plane = me % 4
    half = my_z // 2
    across = my_z * 4 + (1 - my_y) * 2 + my_c
    sibling = my_z * 4 + my_y * 2 + (1 - my_c)
    base = half * (n // 2) if split else 0

    def rows_of(first, count=1):
        return pl.ds(pl.multiple_of(first * ROWS, 8), count * ROWS)

    def slots_of(d):
        return pl.ds(d * cap, cap)

    def page_ends(kind, peer, writer):
        if kind == META:
            return meta_ref.at[peer], meta_out.at[writer]
        if kind == KEYS:
            return pk_ref.at[slots_of(peer - base)], store_k.at[slots_of(writer)]
        return pv_ref.at[slots_of(peer - base)], store_v.at[slots_of(writer)]

    def page(kind, peer, arriving=False):
        src, dst = page_ends(kind, me if arriving else peer, peer if arriving else me)
        return pltpu.make_async_remote_copy(
            src_ref=src, dst_ref=dst, send_sem=page_send.at[kind, peer],
            recv_sem=page_recv.at[kind, peer if arriving else me],
            device_id={"seq": peer}, device_id_type=MESH,
        )

    def row_ends(kind, z, writer):
        if kind == QROW:
            return q_ref, qbuf.at[:, rows_of((my_c * 2 + my_y) * depth + writer), :]
        if kind == PART:
            return obuf2.at[:, rows_of(z), :], pbuf.at[writer]
        return stat2.at[rows_of(z), :], sbuf.at[writer]

    def row(kind, z, arriving=False):
        src, dst = row_ends(kind, z, z if arriving else my_z)
        return pltpu.make_async_remote_copy(
            src_ref=src, dst_ref=dst, send_sem=row_send.at[kind, z],
            recv_sem=row_recv.at[kind, z if arriving else my_z],
            device_id={"seq": z * 4 + my_y * 2 + my_c}, device_id_type=MESH,
        )

    def pair(number, src, dst, peer):
        return pltpu.make_async_remote_copy(
            src_ref=src, dst_ref=dst, send_sem=pair_send.at[number], recv_sem=pair_recv.at[number],
            device_id={"seq": peer}, device_id_type=MESH,
        )

    def own_page(kind):
        src, dst = page_ends(kind, me, me)
        return pltpu.make_async_copy(src, dst, local.at[kind])

    def own_row(kind):
        src, dst = row_ends(kind, my_z, my_z)
        return pltpu.make_async_copy(src, dst, local.at[3 + kind])

    def each(count, mine, body):
        def step(i, _):
            body(lax.rem(mine + i, count))
            return 0

        lax.fori_loop(1, count, step, 0)

    caches = [
        pltpu.make_async_copy(ck_hbm, ck_ref, local.at[6]),
        pltpu.make_async_copy(cv_hbm, cv_ref, local.at[7]),
    ]
    for load in caches:
        load.start()

    barrier = pltpu.get_barrier_semaphore()

    def greet(peer):
        pl.semaphore_signal(barrier, inc=1, device_id={"seq": peer}, device_id_type=MESH)

    def greet_group(g):
        pl.semaphore_signal(barrier, inc=1, device_id={"groups": g}, device_id_type=MESH)

    each(n, me, greet)
    if split:
        each(groups, my_g, greet_group)
    pl.semaphore_wait(barrier, n - 1 + (groups - 1 if split else 0))

    if split:
        pieces = pieces_of(parts)
        mine_near = my_z == 1 + half
        other = (1 - half) * 2
        HEAD, TAIL = 0, 1
        spans = (pl.ds(0, dense - tail), pl.ds(dense - tail, tail))

        def cross(piece, end, zi):
            kind, col, width = pieces[piece]
            src = mk_ref if kind == KEYS else mv_ref
            return pltpu.make_async_remote_copy(
                src_ref=src.at[spans[end], :, pl.ds(col, width)],
                dst_ref=lands[piece].at[zi, spans[end]],
                send_sem=cross_send.at[piece, end], recv_sem=cross_recv.at[piece, end, zi],
                device_id={"seq": (2 - half) * 4 + plane}, device_id_type=MESH,
            )

        def hand(piece, zi):
            buf = lands[piece]
            return pltpu.make_async_remote_copy(
                src_ref=buf.at[zi, spans[TAIL]], dst_ref=buf.at[zi, pl.ds(0, tail)],
                send_sem=pass_send.at[piece, zi], recv_sem=pass_recv.at[piece, zi],
                device_id={"seq": 3 * half * 4 + plane}, device_id_type=MESH,
            )

        def fan(piece, zi, to, writer):
            kind, col, width = pieces[piece]
            src = fan_k if kind == KEYS else fan_v
            dst = store_k if kind == KEYS else store_v
            cols = pl.ds(col, width)
            shard = (other + zi) * 4 + writer
            return pltpu.make_async_remote_copy(
                src_ref=src.at[zi, to, :, :, cols], dst_ref=dst.at[slots_of(shard), :, cols],
                send_sem=fan_send.at[piece, zi, to], recv_sem=fan_recv.at[piece, zi, writer],
                device_id={"seq": my_z * 4 + to}, device_id_type=MESH,
            )

        def launch(piece, end):
            cross(piece, end, my_z % 2).start()

        def pass_on(piece):
            @pl.when(mine_near)
            def _():
                for zi in range(2):
                    cross(piece, TAIL, zi).wait_recv()
                    hand(piece, zi).start()

        def unpack(piece):
            kind, col, width = pieces[piece]
            buf = lands[piece]
            out = fan_k if kind == KEYS else fan_v
            keep = store_k if kind == KEYS else store_v
            cols = pl.ds(col, width)

            @pl.when(mine_near)
            def _():
                for zi in range(2):
                    cross(piece, HEAD, zi).wait_recv()

            @pl.when(jnp.logical_not(mine_near))
            def _():
                for zi in range(2):
                    hand(piece, zi).wait_recv()

            for zi in range(2):
                shard = (other + zi) * 4 + plane

                def page_at(to, k):
                    at = meta_s[shard, ROUTE, to * cap + k]
                    there = jnp.full((PAGE, width), at, jnp.int32) >= 0
                    return jnp.where(
                        there, buf[zi, jnp.maximum(at, 0)], jnp.zeros((), buf.dtype)
                    )

                def send(to):
                    for k in range(cap):
                        out[zi, to, k, :, cols] = page_at(to, k)
                    fan(piece, zi, to, plane).start()

                each(4, plane, send)
                for k in range(cap):
                    keep[shard * cap + k, :, cols] = page_at(plane, k)

    each(depth, my_z, lambda z: row(QROW, z).start())
    own_row(QROW).start()
    each(n, me, lambda peer: page(META, peer).start())
    for kind in (META, KEYS, VALUES):
        own_page(kind).start()

    def start_pages(peer):
        page(KEYS, peer).start()
        page(VALUES, peer).start()

    if split:
        first = half * 2
        other_z = first + (1 - my_z % 2)
        order = [(p, TAIL) for p in range(len(pieces))] + [(p, HEAD) for p in range(len(pieces))]
        late = [(p, HEAD) for p in range(parts, 2 * parts)]
        for item in order:
            if item not in late:
                launch(*item)
        start_pages(other_z * 4 + plane)
        start_pages(other_z * 4 + my_y * 2 + (1 - my_c))
    else:
        def near(i, _):
            z = lax.rem(my_z + depth // 2 + i, depth)

            @pl.when(z != my_z)
            def _():
                start_pages(z * 4 + my_y * 2 + my_c)
                start_pages(z * 4 + my_y * 2 + (1 - my_c))

            return 0

        lax.fori_loop(0, depth, near, 0)

    own_row(QROW).wait()
    each(depth, my_z, lambda z: row(QROW, z, True).wait_recv())
    q_y_out = qbuf.at[:, rows_of((my_c * 2 + my_y) * depth, depth), :]
    q_y_in = qbuf.at[:, rows_of((my_c * 2 + 1 - my_y) * depth, depth), :]
    pair(0, q_y_out, q_y_out, across).start()
    pair(0, q_y_out, q_y_in, across).wait_recv()
    q_c_out = qbuf.at[:, rows_of(my_c * 2 * depth, 2 * depth), :]
    q_c_in = qbuf.at[:, rows_of((1 - my_c) * 2 * depth, 2 * depth), :]
    pair(1, q_c_out, q_c_out, sibling).start()
    own_page(META).wait()
    each(n, me, lambda peer: page(META, peer, True).wait_recv())
    table = pltpu.make_async_copy(meta_out, meta_s, local.at[8])
    table.start()
    if split:
        def share(g, arriving=False):
            return pltpu.make_async_remote_copy(
                src_ref=meta_out, dst_ref=meta_x.at[g if arriving else my_g],
                send_sem=x_send.at[g], recv_sem=x_recv.at[g if arriving else my_g],
                device_id={"groups": g}, device_id_type=MESH,
            )

        each(groups, my_g, lambda g: share(g).start())
    table.wait()

    live = PAGE * counts[me]
    start = PAGE * lax.fori_loop(
        0, n, lambda i, sofar: sofar + jnp.where(i < me, counts[i], 0), jnp.int32(0)
    )
    prompt = PAGE * lax.fori_loop(0, n, lambda i, sofar: sofar + counts[i], jnp.int32(0))

    def set_limit(p, _):
        d = (p % depth) * 4 + ((p // depth) % 2) * 2 + p // (2 * depth)
        at = pl.multiple_of(p * ROWS, 8)
        reach = jnp.minimum(live, meta_s[d, ROUTE, 4 * cap] - start)
        limit[pl.ds(at, 8), :] = jnp.full(
            (8, LANES), jnp.minimum(live, prompt - n + d + 1 - start)
        )
        for s in range(STEPS):
            limit[pl.ds(pl.multiple_of(at + 8 * (s + 1), 8), 8), :] = jnp.full((8, LANES), reach)
        return 0

    lax.fori_loop(0, n, set_limit, 0)
    pair(1, q_c_out, q_c_in, sibling).wait_recv()
    for load in caches:
        load.wait()

    def far(i, _):
        z = lax.rem(my_z + depth // 2 + i, depth)
        start_pages(z * 4 + (1 - my_y) * 2 + my_c)
        start_pages(z * 4 + (1 - my_y) * 2 + (1 - my_c))
        return 0

    if split:
        start_pages(other_z * 4 + (1 - my_y) * 2 + my_c)
        start_pages(other_z * 4 + (1 - my_y) * 2 + (1 - my_c))
    else:
        far(0, 0)

    lane = lax.broadcasted_iota(jnp.int32, (chunk, LANES), 1)
    keys = ck_ref.shape[0]

    def attend(c, _):
        rows = pl.ds(pl.multiple_of(c * chunk, 16), chunk)

        def head(g, stats):
            cols = pl.ds(pl.multiple_of(g * HD, HD), HD)
            scores = lax.dot_general(
                qbuf[g, rows, :], ck_ref[:, cols], (((1,), (1,)), ((), ())),
                preferred_element_type=jnp.float32,
            ) * SCALE
            place = lax.broadcasted_iota(jnp.int32, (chunk, keys), 1)
            bound = limit[rows, 0:1]
            scores = jnp.where(place < bound, scores, MASKED)
            high = jnp.max(scores, axis=1, keepdims=True)
            weights = jnp.exp(scores - high)
            total = jnp.sum(weights, axis=1, keepdims=True)
            summed = jnp.dot(
                weights.astype(jnp.bfloat16), cv_ref[:, cols], preferred_element_type=jnp.float32
            )
            obuf[g, rows, :] = (summed / total).astype(jnp.bfloat16)
            level = jnp.where(bound > 0, high + jnp.log(total), MASKED)
            return jnp.where(lane == g, level, stats)

        stat[rows, :] = lax.fori_loop(0, KVH, head, jnp.zeros((chunk, LANES), jnp.float32))
        return 0

    lax.fori_loop(0, stat.shape[0] // chunk, attend, 0)

    def merge(a, a_stat, first, b, b_stat, to, to_stat):
        step = 2 * ROWS

        def some(i, _):
            here = pl.ds(pl.multiple_of(i * step, 16), step)
            there = pl.ds(pl.multiple_of(first * ROWS + i * step, 16), step)
            one, two = a_stat[there, :], b_stat[here, :]
            high = jnp.maximum(one, two)
            one, two = jnp.exp(one - high), jnp.exp(two - high)
            both = one + two
            to_stat[here, :] = high + jnp.log(both)
            one, two = one / both, two / both
            for g in range(KVH):
                to[g, here, :] = (
                    one[:, g : g + 1] * a[g, there, :].astype(jnp.float32)
                    + two[:, g : g + 1] * b[g, here, :].astype(jnp.float32)
                ).astype(jnp.bfloat16)
            return 0

        lax.fori_loop(0, to_stat.shape[0] // step, some, 0)

    give = (1 - my_c) * 2 * depth
    part1 = pair(2, obuf.at[:, rows_of(give, 2 * depth), :], got1, sibling)
    part1s = pair(3, stat.at[rows_of(give, 2 * depth), :], got1s, sibling)
    part1s.start()
    part1.start()
    if split:
        for piece in range(parts):
            pass_on(piece)
    part1s.wait_recv()
    part1.wait_recv()
    merge(obuf, stat, my_c * 2 * depth, got1, got1s, obuf1, stat1)
    give = (1 - my_y) * depth
    part2 = pair(4, obuf1.at[:, rows_of(give, depth), :], got2, across)
    part2s = pair(5, stat1.at[rows_of(give, depth), :], got2s, across)
    part2s.start()
    part2.start()
    start_pages(sibling)

    own_lane = lax.broadcasted_iota(jnp.int32, (ROWS, LANES), 1)
    own_place = lax.broadcasted_iota(jnp.int32, (ROWS, LANES), 0)
    own_levels = []
    for t in range(STEPS):
        level = jnp.zeros((ROWS, LANES), jnp.float32)
        for g in range(KVH):
            key = ok_ref[t : t + 1, g * HD : (g + 1) * HD].astype(jnp.float32)
            score = jnp.sum(q_ref[g].astype(jnp.float32) * key, axis=1, keepdims=True) * SCALE
            level = jnp.where(own_lane == g, score, level)
        own_levels.append(jnp.where(own_place >= GROUP * (t + 1), level, MASKED))

    part2s.wait_recv()
    part2.wait_recv()
    merge(obuf1, stat1, my_y * depth, got2, got2s, obuf2, stat2)

    def start_rows(z):
        row(STAT, z).start()
        row(PART, z).start()

    each(depth, my_z, start_rows)
    own_row(STAT).start()
    own_row(PART).start()

    if split:
        for item in late:
            launch(*item)
        start_pages(my_z * 4 + (1 - my_y) * 2 + my_c)
        start_pages(my_z * 4 + (1 - my_y) * 2 + (1 - my_c))
        for piece in range(parts, 2 * parts):
            pass_on(piece)
        for piece in range(parts):
            unpack(piece)
    else:
        lax.fori_loop(1, depth, far, 0)

    own_row(STAT).wait()
    own_row(PART).wait()

    def wait_rows(z):
        row(STAT, z, True).wait_recv()
        row(PART, z, True).wait_recv()

    each(depth, my_z, wait_rows)

    top = functools.reduce(jnp.maximum, own_levels)
    top = lax.fori_loop(0, depth, lambda d, high: jnp.maximum(high, sbuf[d]), top)

    norm = jnp.zeros((ROWS, LANES), jnp.float32)
    sums = [jnp.zeros((ROWS, HD), jnp.float32) for _ in range(KVH)]
    for t in range(STEPS):
        factor = jnp.exp(own_levels[t] - top)
        norm = norm + factor
        for g in range(KVH):
            value = ov_ref[t : t + 1, g * HD : (g + 1) * HD].astype(jnp.float32)
            sums[g] = sums[g] + factor[:, g : g + 1] * value

    def add(d, state):
        norm, sums = state
        factor = jnp.exp(sbuf[d] - top)
        sums = tuple(
            sums[g] + factor[:, g : g + 1] * pbuf[d, g].astype(jnp.float32) for g in range(KVH)
        )
        return norm + factor, sums

    norm, sums = lax.fori_loop(0, depth, add, (norm, tuple(sums)))
    for g in range(KVH):
        result = (sums[g] / norm[:, g : g + 1]).astype(pre_out.dtype)
        for h in range(GROUP):
            at = (g * GROUP + h) * HD
            pre_out[0:1, at : at + HD] = result[h : h + 1]
            for s in range(STEPS):
                r = (s + 1) * GROUP + h
                dec_out[s : s + 1, at : at + HD] = result[r : r + 1]

    if split:
        for piece in range(parts, 2 * parts):
            unpack(piece)
        each(groups, my_g, lambda g: share(g, True).wait_recv())
        tables = pltpu.make_async_copy(meta_x, meta_xs, local.at[9])
        tables.start()
        tables.wait()

        def worst(i, sofar):
            return jnp.maximum(sofar, meta_s[i, ROUTE, 4 * cap + 1])

        over = lax.fori_loop(0, n, worst, jnp.int32(0))
        for other_g in range(groups):
            def worse(i, sofar):
                return jnp.maximum(
                    sofar, jnp.where(my_g == other_g, 0, meta_xs[other_g, i, ROUTE, 4 * cap + 1])
                )

            over = lax.fori_loop(0, n, worse, over)
        flag_out[0] = over

    pair(0, q_y_out, q_y_out, across).wait_send()
    pair(1, q_c_out, q_c_out, sibling).wait_send()
    for copy in (part1, part1s, part2, part2s):
        copy.wait_send()

    def finish_row(z):
        for kind in (QROW, PART, STAT):
            row(kind, z).wait_send()

    each(depth, my_z, finish_row)
    own_page(KEYS).wait()
    own_page(VALUES).wait()
    each(n, me, lambda peer: page(META, peer).wait_send())

    def finish(peer):
        page(KEYS, peer, True).wait_recv()
        page(VALUES, peer, True).wait_recv()
        for kind in (KEYS, VALUES):
            page(kind, peer).wait_send()

    if split:
        each(groups, my_g, lambda g: share(g).wait_send())
        each(n // 2, me - base, lambda i: finish(base + i))
        for item in order:
            cross(*item, my_z % 2).wait_send()
        for piece in range(2 * parts):
            @pl.when(mine_near)
            def _():
                for zi in range(2):
                    hand(piece, zi).wait_send()

            for zi in range(2):
                def settle(to):
                    fan(piece, zi, to, plane).wait_send()
                    fan(piece, zi, to, to).wait_recv()

                each(4, plane, settle)
    else:
        each(n, me, finish)


def main(n, cap, split, groups, counts, q, meta, ck, cv, pk, pv, own_k, own_v, cross):
    height = n * ROWS
    chunk = min(height, 384)
    _, dense, tail = plan(n, cap)
    parts_count = 2
    vmem = pl.BlockSpec(memory_space=pltpu.VMEM)
    smem = pl.BlockSpec(memory_space=pltpu.SMEM)
    hbm = pl.BlockSpec(memory_space=pltpu.HBM)

    def parts(rows):
        return pltpu.VMEM((KVH, rows, HD), jnp.bfloat16)

    def stats(rows):
        return pltpu.VMEM((rows, LANES), jnp.float32)

    half, quarter, depth = height // 2, height // 4, n // 4
    store = (n * cap, PAGE, KVD)
    out_shape = [
        jax.ShapeDtypeStruct((1, HQ * HD), q.dtype),
        jax.ShapeDtypeStruct((STEPS, HQ * HD), q.dtype),
        jax.ShapeDtypeStruct(store, pk.dtype),
        jax.ShapeDtypeStruct(store, pv.dtype),
        jax.ShapeDtypeStruct(meta.shape, meta.dtype),
    ]
    out_specs = [vmem] * 5
    scratch = [
        pltpu.VMEM(ck.shape, ck.dtype), pltpu.VMEM(cv.shape, cv.dtype),
        pltpu.SMEM(meta.shape, jnp.int32),
        parts(height), parts(height), stats(height), pltpu.VMEM((height, LANES), jnp.int32),
        parts(half), stats(half), parts(half), stats(half),
        parts(quarter), stats(quarter), parts(quarter), stats(quarter),
        pltpu.VMEM((depth, KVH, ROWS, HD), jnp.bfloat16),
        pltpu.VMEM((depth, ROWS, LANES), jnp.float32),
        pltpu.SemaphoreType.DMA((3, n)),
        pltpu.SemaphoreType.DMA((3, n)),
        pltpu.SemaphoreType.DMA((3, depth)),
        pltpu.SemaphoreType.DMA((3, depth)),
        pltpu.SemaphoreType.DMA((6,)),
        pltpu.SemaphoreType.DMA((6,)),
        pltpu.SemaphoreType.DMA((10,)),
    ]
    if split:
        out_shape.append(jax.ShapeDtypeStruct((1,), jnp.int32))
        out_specs.append(smem)
        count = 2 * parts_count
        scratch += [
            pltpu.VMEM((groups,) + meta.shape, jnp.int32),
            pltpu.SMEM((groups,) + meta.shape, jnp.int32),
            *[pltpu.VMEM((2, dense, PAGE, w), pk.dtype) for _, _, w in pieces_of(parts_count)],
            pltpu.VMEM((2, 4, cap, PAGE, KVD), pk.dtype),
            pltpu.VMEM((2, 4, cap, PAGE, KVD), pv.dtype),
            pltpu.SemaphoreType.DMA((groups,)),
            pltpu.SemaphoreType.DMA((groups,)),
            pltpu.SemaphoreType.DMA((count, 2)),
            pltpu.SemaphoreType.DMA((count, 2, 2)),
            pltpu.SemaphoreType.DMA((count, 2)),
            pltpu.SemaphoreType.DMA((count, 2)),
            pltpu.SemaphoreType.DMA((count, 2, 4)),
            pltpu.SemaphoreType.DMA((count, 2, 4)),
        ]
    return pl.pallas_call(
        functools.partial(main_kernel, n, cap, chunk, split, dense, tail, parts_count),
        in_specs=[smem] + [vmem] * 2 + [hbm] * 2 + [vmem] * (4 + len(cross)),
        out_specs=out_specs,
        out_shape=out_shape,
        scratch_shapes=scratch,
        compiler_params=pltpu.CompilerParams(
            collective_id=0, has_side_effects=True, vmem_limit_bytes=32 << 20
        ),
        name="exchange",
    )(counts, q, meta, ck, cv, pk, pv, own_k, own_v, *cross)


def direct_kernel(n, cap, pk_ref, pv_ref, store_k, store_v, send, recv, local):
    me = lax.axis_index("seq")

    def slots_of(d):
        return pl.ds(d * cap, cap)

    def ends(kind, to, writer):
        src, dst = (pk_ref, store_k) if kind == 0 else (pv_ref, store_v)
        return src.at[slots_of(to)], dst.at[slots_of(writer)]

    def page(kind, peer, arriving=False):
        src, dst = ends(kind, peer, peer if arriving else me)
        return pltpu.make_async_remote_copy(
            src_ref=src, dst_ref=dst, send_sem=send.at[kind, peer],
            recv_sem=recv.at[kind, peer if arriving else me],
            device_id={"seq": peer}, device_id_type=MESH,
        )

    def each(body):
        def step(i, _):
            body(lax.rem(me + i, n))
            return 0

        lax.fori_loop(1, n, step, 0)

    barrier = pltpu.get_barrier_semaphore()
    each(
        lambda peer: pl.semaphore_signal(
            barrier, inc=1, device_id={"seq": peer}, device_id_type=MESH
        )
    )
    pl.semaphore_wait(barrier, n - 1)
    own = []
    for kind in range(2):
        each(lambda peer: page(kind, peer).start())
        src, dst = ends(kind, me, me)
        own.append(pltpu.make_async_copy(src, dst, local.at[kind]))
        own[-1].start()
    for kind in range(2):
        own[kind].wait()
        each(lambda peer: page(kind, peer, True).wait_recv())
        each(lambda peer: page(kind, peer).wait_send())


def direct(n, cap, pk, pv):
    vmem = pl.BlockSpec(memory_space=pltpu.VMEM)
    return pl.pallas_call(
        functools.partial(direct_kernel, n, cap),
        in_specs=[vmem] * 2,
        out_specs=[vmem] * 2,
        out_shape=[jax.ShapeDtypeStruct(x.shape, x.dtype) for x in (pk, pv)],
        scratch_shapes=[
            pltpu.SemaphoreType.DMA((2, n)),
            pltpu.SemaphoreType.DMA((2, n)),
            pltpu.SemaphoreType.DMA((2,)),
        ],
        compiler_params=pltpu.CompilerParams(
            collective_id=1, has_side_effects=True, vmem_limit_bytes=16 << 20
        ),
        name="direct",
    )(pk, pv)


def write_kernel(
    n, cap, k_in, v_in, pre_in, dec_in, meta_in,
    k_out, v_out, pre_out, dec_out, ids_out, ids, done,
):
    copies = [
        pltpu.make_async_copy(k_in, k_out, done.at[0]),
        pltpu.make_async_copy(v_in, v_out, done.at[1]),
        pltpu.make_async_copy(pre_in, pre_out, done.at[2]),
        pltpu.make_async_copy(dec_in, dec_out, done.at[3]),
    ]
    for copy in copies:
        copy.start()
    lane = lax.broadcasted_iota(jnp.int32, (1, n * cap), 1)
    row = meta_in[0, IDS : IDS + 1, :]
    for s in range(1, n):
        row = jnp.where(lane // cap == s, meta_in[s, IDS : IDS + 1, :], row)
    ids[...] = row
    last = pltpu.make_async_copy(ids, ids_out, done.at[4])
    last.start()
    for copy in copies + [last]:
        copy.wait()


def write(n, cap, store_k, store_v, pre, dec, meta):
    vmem = pl.BlockSpec(memory_space=pltpu.VMEM)
    hbm = pl.BlockSpec(memory_space=pltpu.HBM)
    return pl.pallas_call(
        functools.partial(write_kernel, n, cap),
        in_specs=[vmem] * 5,
        out_specs=[hbm] * 5,
        out_shape=[jax.ShapeDtypeStruct(x.shape, x.dtype) for x in (store_k, store_v, pre, dec)]
        + [jax.ShapeDtypeStruct((1, n * cap), jnp.int32)],
        scratch_shapes=[pltpu.VMEM((1, n * cap), jnp.int32), pltpu.SemaphoreType.DMA((5,))],
        compiler_params=pltpu.CompilerParams(vmem_limit_bytes=16 << 20),
        name="write",
    )(store_k, store_v, pre, dec, meta)


def per_device(
    prefill_q, cache_k, cache_v, page_counts, page_owner, decode_q, decode_k, decode_v, context_len
):
    n = lax.axis_size("seq")
    groups = lax.axis_size("groups")
    page_slots = cache_k.shape[0] // PAGE
    cap = max(2, 2 * page_slots // n)
    split, _, _ = plan(n, cap)
    ck = cache_k.reshape(page_slots, PAGE, KVD)
    cv = cache_v.reshape(page_slots, PAGE, KVD)
    owner = page_owner[:, 0]
    parts = (page_counts, context_len, ck, cv, prefill_q, decode_q[0])
    pk, pv, *cross, q, meta = prep(n, cap, split, owner, *parts)
    pre, dec, store_k, store_v, meta, *flag = main(
        n, cap, split, groups, page_counts, q, meta, cache_k, cache_v, pk, pv,
        decode_k[0], decode_v[0], cross,
    )

    def keep(sk, sv, pre, dec, meta):
        return write(n, cap, sk, sv, pre, dec, meta)

    def again(sk, sv, pre, dec, meta):
        pk, pv, _, _ = prep(n, cap, False, owner, *parts)
        sk, sv = direct(n, cap, pk, pv)
        return write(n, cap, sk, sv, pre, dec, meta)

    if split:
        results = lax.cond(flag[0][0] > 0, again, keep, store_k, store_v, pre, dec, meta)
    else:
        results = keep(store_k, store_v, pre, dec, meta)
    store_k, store_v, pre, dec, ids = results
    return (
        pre,
        dec.reshape(1, STEPS, HQ * HD),
        store_k.reshape(-1, KVD),
        store_v.reshape(-1, KVD),
        ids.reshape(-1),
    )


def solution(mesh):
    both = ("groups", "seq")
    in_specs = (
        P(both, None),
        P(both, None),
        P(both, None),
        P("groups"),
        P(both, None),
        P(both, None, None),
        P(both, None, None),
        P(both, None, None),
        P(both),
    )
    out_specs = (
        P(both, None),
        P(both, None, None),
        P(both, None),
        P(both, None),
        P(both),
    )
    return jax.shard_map(
        per_device, mesh=mesh, in_specs=in_specs, out_specs=out_specs, check_vma=False
    )
```

```python
import functools

import jax
import jax.numpy as jnp
from jax import lax
from jax.experimental import pallas as pl
from jax.experimental.pallas import tpu as pltpu
from jax.sharding import PartitionSpec as P

HQ = 64
KVH = 8
HD = 128
PAGE = 8
STEPS = 2
KVD = 1024
GROUP = HQ // KVH
ROWS = (1 + STEPS) * GROUP
LANES = 128
MASKED = -1e30
SCALE = HD ** (-0.5)
MESH = pl.DeviceIdType.MESH

META, KEYS, VALUES = range(3)
QROW, PART, STAT = range(3)
IDS, ROUTE = range(2)


def plan(n, cap):
    if n // 4 != 4 or n % 4:
        return False, 0, 0
    most = cap * n // 2
    return True, most * 11 // 16, most // 2 * 7 // 8


def pieces_of(parts):
    width = KVD // parts
    return [(kind, i * width, width) for kind in (KEYS, VALUES) for i in range(parts)]


def prep_kernel(
    n, cap, page_slots, split, dense, tail,
    owner, counts, context, ck_hbm, cv_hbm, pq, dq,
    out_k, out_v, *rest,
):
    if split:
        cross_k, cross_v, q_out, meta, ck, cv, table, seen, cross, tally, done = rest
    else:
        q_out, meta, ck, cv, table, seen, done = rest
    me = lax.axis_index("seq")
    my_z, plane = me // 4, me % 4
    half = my_z // 2
    span = n // 2 if split else n
    base = half * span if split else 0
    loads = [
        pltpu.make_async_copy(ck_hbm, ck, done.at[0]),
        pltpu.make_async_copy(cv_hbm, cv, done.at[1]),
    ]
    for load in loads:
        load.start()

    for s in range(1 + STEPS):
        for h in range(HQ):
            row = s * GROUP + h % GROUP
            src = pq if s == 0 else dq
            at = 0 if s == 0 else s - 1
            q_out[h // GROUP, row : row + 1, :] = src[at : at + 1, h * HD : (h + 1) * HD]

    def clear(i, _):
        seen[i] = 0
        for k in range(cap):
            table[i * cap + k] = -1
            meta[i, IDS, me * cap + k] = -1
        meta[i, ROUTE, 4 * cap] = context[0]
        return 0

    lax.fori_loop(0, n, clear, 0)
    if split:
        near = (2 - half) * 4 + plane
        far = 3 * (1 - half) * 4 + plane
        for k in range(4 * cap):
            meta[near, ROUTE, k] = -1
            meta[far, ROUTE, k] = -1

        def zero(i, _):
            cross[i] = 0
            return 0

        lax.fori_loop(0, dense, zero, 0)
        tally[0] = 0
        tally[1] = 0
        tally[2] = 0

    def place(j, _):
        o = owner[j]
        k = seen[o]
        seen[o] = k + 1
        table[o * cap + k] = j
        meta[o, IDS, me * cap + k] = me * page_slots + j
        if split:
            @pl.when(o // 4 // 2 != half)
            def _():
                front, back = tally[0], tally[1]
                room = front + back < dense
                at = (o % 4) * cap + k

                @pl.when(room & (o // 4 == 2 - half))
                def _():
                    cross[front] = j
                    meta[near, ROUTE, at] = front
                    tally[0] = front + 1

                fits = room & (back < tail)

                @pl.when(fits & (o // 4 != 2 - half))
                def _():
                    cross[dense - 1 - back] = j
                    meta[far, ROUTE, at] = tail - 1 - back
                    tally[1] = back + 1

                @pl.when(jnp.logical_not(jnp.where(o // 4 == 2 - half, room, fits)))
                def _():
                    tally[2] = 1

        return 0

    lax.fori_loop(0, counts[me], place, 0)

    if split:
        def flag(i, _):
            meta[i, ROUTE, 4 * cap + 1] = tally[2]
            return 0

        lax.fori_loop(0, n, flag, 0)

    for load in loads:
        load.wait()

    if split:
        def pick(i, _):
            page = cross[i]
            cross_k[i] = ck[page]
            cross_v[i] = cv[page]
            return 0

        lax.fori_loop(0, dense, pick, 0)

    def fill(i, _):
        for k in range(cap):
            src = table[(base + i) * cap + k]
            page = jnp.maximum(src, 0)
            there = jnp.full((PAGE, KVD), src, jnp.int32) >= 0
            out_k[i * cap + k] = jnp.where(there, ck[page], jnp.zeros((), out_k.dtype))
            out_v[i * cap + k] = jnp.where(there, cv[page], jnp.zeros((), out_v.dtype))
        return 0

    lax.fori_loop(0, span, fill, 0)


def prep(n, cap, split, owner, counts, context, ck, cv, pq, dq):
    page_slots = ck.shape[0]
    _, dense, tail = plan(n, cap)
    smem = pl.BlockSpec(memory_space=pltpu.SMEM)
    vmem = pl.BlockSpec(memory_space=pltpu.VMEM)
    hbm = pl.BlockSpec(memory_space=pltpu.HBM)
    span = n // 2 if split else n

    def pages(count):
        return [jax.ShapeDtypeStruct((count, PAGE, KVD), x.dtype) for x in (ck, cv)]

    out_shape = pages(span * cap) + (pages(dense) if split else [])
    out_specs = [vmem] * len(out_shape) + [vmem, smem]
    out_shape += [
        jax.ShapeDtypeStruct((KVH, ROWS, HD), pq.dtype),
        jax.ShapeDtypeStruct((n, 2, n * cap), jnp.int32),
    ]
    scratch = [
        pltpu.VMEM(ck.shape, ck.dtype), pltpu.VMEM(cv.shape, cv.dtype),
        pltpu.SMEM((n * cap,), jnp.int32), pltpu.SMEM((n,), jnp.int32),
    ]
    if split:
        scratch += [pltpu.SMEM((dense,), jnp.int32), pltpu.SMEM((4,), jnp.int32)]
    return pl.pallas_call(
        functools.partial(prep_kernel, n, cap, page_slots, split, dense, tail),
        in_specs=[smem, smem, smem, hbm, hbm, vmem, vmem],
        out_specs=out_specs,
        out_shape=out_shape,
        scratch_shapes=scratch + [pltpu.SemaphoreType.DMA((2,))],
        compiler_params=pltpu.CompilerParams(vmem_limit_bytes=16 << 20),
        name="prep",
    )(owner, counts, context, ck, cv, pq, dq)


def main_kernel(
    n, cap, chunk, split, dense, tail, parts,
    counts, q_ref, meta_ref, ck_hbm, cv_hbm, pk_ref, pv_ref, ok_ref, ov_ref, *rest,
):
    if split:
        mk_ref, mv_ref = rest[:2]
        rest = rest[2:]
    pre_out, dec_out, store_k, store_v, meta_out = rest[:5]
    rest = rest[5:]
    if split:
        flag_out = rest[0]
        rest = rest[1:]
    (
        ck_ref, cv_ref, meta_s,
        qbuf, obuf, stat, limit, got1, got1s, obuf1, stat1, got2, got2s, obuf2, stat2, pbuf, sbuf,
        page_send, page_recv, row_send, row_recv, pair_send, pair_recv, local,
    ) = rest[:24]
    rest = rest[24:]
    if split:
        (
            meta_x, meta_xs, *lands, fan_k, fan_v,
            x_send, x_recv, cross_send, cross_recv, pass_send, pass_recv, fan_send, fan_recv,
        ) = rest
    depth = n // 4
    groups = lax.axis_size("groups")
    my_g = lax.axis_index("groups")
    me = lax.axis_index("seq")
    my_z, my_y, my_c = me // 4, (me // 2) % 2, me % 2
    plane = me % 4
    half = my_z // 2
    across = my_z * 4 + (1 - my_y) * 2 + my_c
    sibling = my_z * 4 + my_y * 2 + (1 - my_c)
    base = half * (n // 2) if split else 0

    def rows_of(first, count=1):
        return pl.ds(pl.multiple_of(first * ROWS, 8), count * ROWS)

    def slots_of(d):
        return pl.ds(d * cap, cap)

    def page_ends(kind, peer, writer):
        if kind == META:
            return meta_ref.at[peer], meta_out.at[writer]
        if kind == KEYS:
            return pk_ref.at[slots_of(peer - base)], store_k.at[slots_of(writer)]
        return pv_ref.at[slots_of(peer - base)], store_v.at[slots_of(writer)]

    def page(kind, peer, arriving=False):
        src, dst = page_ends(kind, me if arriving else peer, peer if arriving else me)
        return pltpu.make_async_remote_copy(
            src_ref=src, dst_ref=dst, send_sem=page_send.at[kind, peer],
            recv_sem=page_recv.at[kind, peer if arriving else me],
            device_id={"seq": peer}, device_id_type=MESH,
        )

    def row_ends(kind, z, writer):
        if kind == QROW:
            return q_ref, qbuf.at[:, rows_of((my_c * 2 + my_y) * depth + writer), :]
        if kind == PART:
            return obuf2.at[:, rows_of(z), :], pbuf.at[writer]
        return stat2.at[rows_of(z), :], sbuf.at[writer]

    def row(kind, z, arriving=False):
        src, dst = row_ends(kind, z, z if arriving else my_z)
        return pltpu.make_async_remote_copy(
            src_ref=src, dst_ref=dst, send_sem=row_send.at[kind, z],
            recv_sem=row_recv.at[kind, z if arriving else my_z],
            device_id={"seq": z * 4 + my_y * 2 + my_c}, device_id_type=MESH,
        )

    def pair(number, src, dst, peer):
        return pltpu.make_async_remote_copy(
            src_ref=src, dst_ref=dst, send_sem=pair_send.at[number], recv_sem=pair_recv.at[number],
            device_id={"seq": peer}, device_id_type=MESH,
        )

    def own_page(kind):
        src, dst = page_ends(kind, me, me)
        return pltpu.make_async_copy(src, dst, local.at[kind])

    def own_row(kind):
        src, dst = row_ends(kind, my_z, my_z)
        return pltpu.make_async_copy(src, dst, local.at[3 + kind])

    def each(count, mine, body):
        def step(i, _):
            body(lax.rem(mine + i, count))
            return 0

        lax.fori_loop(1, count, step, 0)

    caches = [
        pltpu.make_async_copy(ck_hbm, ck_ref, local.at[6]),
        pltpu.make_async_copy(cv_hbm, cv_ref, local.at[7]),
    ]
    for load in caches:
        load.start()

    barrier = pltpu.get_barrier_semaphore()

    def greet(peer):
        pl.semaphore_signal(barrier, inc=1, device_id={"seq": peer}, device_id_type=MESH)

    def greet_group(g):
        pl.semaphore_signal(barrier, inc=1, device_id={"groups": g}, device_id_type=MESH)

    each(n, me, greet)
    if split:
        each(groups, my_g, greet_group)
    pl.semaphore_wait(barrier, n - 1 + (groups - 1 if split else 0))

    if split:
        pieces = pieces_of(parts)
        inner = my_z == 1 + half
        other = (1 - half) * 2
        by_inner, by_outer = half, 1 - half
        keys_at, values_at = range(parts), range(parts, 2 * parts)
        HEAD, TAIL = 0, 1
        INNER, OUTER = 0, 1
        lands = lands[: len(pieces)], lands[len(pieces) :]
        spans = (pl.ds(0, dense - tail), pl.ds(dense - tail, tail))

        def cross(piece, end, side):
            kind, col, width = pieces[piece]
            src = mk_ref if kind == KEYS else mv_ref
            return pltpu.make_async_remote_copy(
                src_ref=src.at[spans[end], :, pl.ds(col, width)],
                dst_ref=lands[side][piece].at[spans[end]],
                send_sem=cross_send.at[piece, end], recv_sem=cross_recv.at[piece, end, side],
                device_id={"seq": (2 - half) * 4 + plane}, device_id_type=MESH,
            )

        def hand(piece, side):
            buf = lands[side][piece]
            return pltpu.make_async_remote_copy(
                src_ref=buf.at[spans[TAIL]], dst_ref=buf.at[pl.ds(0, tail)],
                send_sem=pass_send.at[piece, side], recv_sem=pass_recv.at[piece, side],
                device_id={"seq": 3 * half * 4 + plane}, device_id_type=MESH,
            )

        def fan(piece, zi, to, writer):
            kind, col, width = pieces[piece]
            src = fan_k if kind == KEYS else fan_v
            dst = store_k if kind == KEYS else store_v
            cols = pl.ds(col, width)
            shard = (other + zi) * 4 + writer
            return pltpu.make_async_remote_copy(
                src_ref=src.at[zi, to, :, :, cols], dst_ref=dst.at[slots_of(shard), :, cols],
                send_sem=fan_send.at[piece, zi, to], recv_sem=fan_recv.at[piece, zi, writer],
                device_id={"seq": my_z * 4 + to}, device_id_type=MESH,
            )

        def launch(items, side):
            for item in items:
                cross(*item, side).start()

        def pass_on(numbers, side):
            @pl.when(inner)
            def _():
                for piece in numbers:
                    cross(piece, TAIL, side).wait_recv()
                    hand(piece, side).start()

        def unpack(piece, side, near):
            kind, col, width = pieces[piece]
            buf = lands[side][piece]
            out = fan_k if kind == KEYS else fan_v
            keep = store_k if kind == KEYS else store_v
            cols = pl.ds(col, width)
            if near:
                cross(piece, HEAD, side).wait_recv()
            else:
                hand(piece, side).wait_recv()
            zi = by_inner if side == INNER else by_outer
            shard = (other + zi) * 4 + plane

            def page_at(to, k):
                at = meta_s[shard, ROUTE, to * cap + k]
                there = jnp.full((PAGE, width), at, jnp.int32) >= 0
                return jnp.where(there, buf[jnp.maximum(at, 0)], jnp.zeros((), buf.dtype))

            def send(to):
                for k in range(cap):
                    out[zi, to, k, :, cols] = page_at(to, k)
                fan(piece, zi, to, plane).start()

            each(4, plane, send)
            for k in range(cap):
                keep[shard * cap + k, :, cols] = page_at(plane, k)

    each(depth, my_z, lambda z: row(QROW, z).start())
    own_row(QROW).start()
    each(n, me, lambda peer: page(META, peer).start())
    for kind in (META, KEYS, VALUES):
        own_page(kind).start()

    if split:
        order = [(p, TAIL) for p in range(2 * parts)] + [(p, HEAD) for p in range(2 * parts)]

        @pl.when(inner)
        def _():
            launch(order[:-parts], INNER)

    def start_pages(peer):
        page(KEYS, peer).start()
        page(VALUES, peer).start()

    own_row(QROW).wait()
    each(depth, my_z, lambda z: row(QROW, z, True).wait_recv())
    own_page(META).wait()
    each(n, me, lambda peer: page(META, peer, True).wait_recv())
    if split:
        first = half * 2
        other_z = first + (1 - my_z % 2)
        @pl.when(jnp.logical_not(inner))
        def _():
            launch(order[:parts], OUTER)

        start_pages(other_z * 4 + plane)
        start_pages(other_z * 4 + my_y * 2 + (1 - my_c))
    else:
        def near(i, _):
            z = lax.rem(my_z + depth // 2 + i, depth)

            @pl.when(z != my_z)
            def _():
                start_pages(z * 4 + my_y * 2 + my_c)
                start_pages(z * 4 + my_y * 2 + (1 - my_c))

            return 0

        lax.fori_loop(0, depth, near, 0)

    q_y_out = qbuf.at[:, rows_of((my_c * 2 + my_y) * depth, depth), :]
    q_y_in = qbuf.at[:, rows_of((my_c * 2 + 1 - my_y) * depth, depth), :]
    pair(0, q_y_out, q_y_out, across).start()
    if split:
        start_pages(my_z * 4 + (1 - my_y) * 2 + my_c)
        start_pages(my_z * 4 + (1 - my_y) * 2 + (1 - my_c))
    pair(0, q_y_out, q_y_in, across).wait_recv()
    q_c_out = qbuf.at[:, rows_of(my_c * 2 * depth, 2 * depth), :]
    q_c_in = qbuf.at[:, rows_of((1 - my_c) * 2 * depth, 2 * depth), :]
    pair(1, q_c_out, q_c_out, sibling).start()
    table = pltpu.make_async_copy(meta_out, meta_s, local.at[8])
    table.start()
    if split:
        def share(g, arriving=False):
            return pltpu.make_async_remote_copy(
                src_ref=meta_out, dst_ref=meta_x.at[g if arriving else my_g],
                send_sem=x_send.at[g], recv_sem=x_recv.at[g if arriving else my_g],
                device_id={"groups": g}, device_id_type=MESH,
            )

        each(groups, my_g, lambda g: share(g).start())
    table.wait()

    live = PAGE * counts[me]
    start = PAGE * lax.fori_loop(
        0, n, lambda i, sofar: sofar + jnp.where(i < me, counts[i], 0), jnp.int32(0)
    )
    prompt = PAGE * lax.fori_loop(0, n, lambda i, sofar: sofar + counts[i], jnp.int32(0))

    def set_limit(p, _):
        d = (p % depth) * 4 + ((p // depth) % 2) * 2 + p // (2 * depth)
        at = pl.multiple_of(p * ROWS, 8)
        reach = jnp.minimum(live, meta_s[d, ROUTE, 4 * cap] - start)
        limit[pl.ds(at, 8), :] = jnp.full(
            (8, LANES), jnp.minimum(live, prompt - n + d + 1 - start)
        )
        for s in range(STEPS):
            limit[pl.ds(pl.multiple_of(at + 8 * (s + 1), 8), 8), :] = jnp.full((8, LANES), reach)
        return 0

    lax.fori_loop(0, n, set_limit, 0)
    pair(1, q_c_out, q_c_in, sibling).wait_recv()
    for load in caches:
        load.wait()

    def far(i, _):
        z = lax.rem(my_z + depth // 2 + i, depth)
        start_pages(z * 4 + (1 - my_y) * 2 + my_c)
        start_pages(z * 4 + (1 - my_y) * 2 + (1 - my_c))
        return 0

    if not split:
        far(0, 0)

    if split:
        pass_on(keys_at, INNER)
    lane = lax.broadcasted_iota(jnp.int32, (chunk, LANES), 1)
    keys = ck_ref.shape[0]

    def attend(c, _):
        rows = pl.ds(pl.multiple_of(c * chunk, 16), chunk)

        def head(g, stats):
            cols = pl.ds(pl.multiple_of(g * HD, HD), HD)
            scores = lax.dot_general(
                qbuf[g, rows, :], ck_ref[:, cols], (((1,), (1,)), ((), ())),
                preferred_element_type=jnp.float32,
            ) * SCALE
            place = lax.broadcasted_iota(jnp.int32, (chunk, keys), 1)
            bound = limit[rows, 0:1]
            scores = jnp.where(place < bound, scores, MASKED)
            high = jnp.max(scores, axis=1, keepdims=True)
            weights = jnp.exp(scores - high)
            total = jnp.sum(weights, axis=1, keepdims=True)
            summed = jnp.dot(
                weights.astype(jnp.bfloat16), cv_ref[:, cols], preferred_element_type=jnp.float32
            )
            obuf[g, rows, :] = (summed / total).astype(jnp.bfloat16)
            level = jnp.where(bound > 0, high + jnp.log(total), MASKED)
            return jnp.where(lane == g, level, stats)

        stat[rows, :] = lax.fori_loop(0, KVH, head, jnp.zeros((chunk, LANES), jnp.float32))
        return 0

    lax.fori_loop(0, stat.shape[0] // chunk, attend, 0)

    def merge(a, a_stat, first, b, b_stat, to, to_stat):
        step = 2 * ROWS

        def some(i, _):
            here = pl.ds(pl.multiple_of(i * step, 16), step)
            there = pl.ds(pl.multiple_of(first * ROWS + i * step, 16), step)
            one, two = a_stat[there, :], b_stat[here, :]
            high = jnp.maximum(one, two)
            one, two = jnp.exp(one - high), jnp.exp(two - high)
            both = one + two
            to_stat[here, :] = high + jnp.log(both)
            one, two = one / both, two / both
            for g in range(KVH):
                to[g, here, :] = (
                    one[:, g : g + 1] * a[g, there, :].astype(jnp.float32)
                    + two[:, g : g + 1] * b[g, here, :].astype(jnp.float32)
                ).astype(jnp.bfloat16)
            return 0

        lax.fori_loop(0, to_stat.shape[0] // step, some, 0)

    give = (1 - my_c) * 2 * depth
    part1 = pair(2, obuf.at[:, rows_of(give, 2 * depth), :], got1, sibling)
    part1s = pair(3, stat.at[rows_of(give, 2 * depth), :], got1s, sibling)
    part1s.start()
    part1.start()
    part1s.wait_recv()
    part1.wait_recv()
    merge(obuf, stat, my_c * 2 * depth, got1, got1s, obuf1, stat1)
    give = (1 - my_y) * depth
    part2 = pair(4, obuf1.at[:, rows_of(give, depth), :], got2, across)
    part2s = pair(5, stat1.at[rows_of(give, depth), :], got2s, across)
    part2s.start()
    part2.start()
    start_pages(sibling)
    if split:
        pass_on(keys_at, OUTER)
        pass_on(values_at, INNER)

    own_lane = lax.broadcasted_iota(jnp.int32, (ROWS, LANES), 1)
    own_place = lax.broadcasted_iota(jnp.int32, (ROWS, LANES), 0)
    own_levels = []
    for t in range(STEPS):
        level = jnp.zeros((ROWS, LANES), jnp.float32)
        for g in range(KVH):
            key = ok_ref[t : t + 1, g * HD : (g + 1) * HD].astype(jnp.float32)
            score = jnp.sum(q_ref[g].astype(jnp.float32) * key, axis=1, keepdims=True) * SCALE
            level = jnp.where(own_lane == g, score, level)
        own_levels.append(jnp.where(own_place >= GROUP * (t + 1), level, MASKED))

    part2s.wait_recv()
    part2.wait_recv()
    merge(obuf1, stat1, my_y * depth, got2, got2s, obuf2, stat2)

    def start_rows(z):
        row(STAT, z).start()
        row(PART, z).start()

    each(depth, my_z, start_rows)
    own_row(STAT).start()
    own_row(PART).start()

    if split:
        @pl.when(inner)
        def _():
            launch(order[-parts:], INNER)

        start_pages(other_z * 4 + (1 - my_y) * 2 + my_c)
        start_pages(other_z * 4 + (1 - my_y) * 2 + (1 - my_c))
    else:
        lax.fori_loop(1, depth, far, 0)

    own_row(STAT).wait()
    own_row(PART).wait()

    def wait_rows(z):
        row(STAT, z, True).wait_recv()
        row(PART, z, True).wait_recv()

    each(depth, my_z, wait_rows)

    if split:
        @pl.when(jnp.logical_not(inner))
        def _():
            launch(order[parts:], OUTER)

    top = functools.reduce(jnp.maximum, own_levels)
    top = lax.fori_loop(0, depth, lambda d, high: jnp.maximum(high, sbuf[d]), top)

    norm = jnp.zeros((ROWS, LANES), jnp.float32)
    sums = [jnp.zeros((ROWS, HD), jnp.float32) for _ in range(KVH)]
    for t in range(STEPS):
        factor = jnp.exp(own_levels[t] - top)
        norm = norm + factor
        for g in range(KVH):
            value = ov_ref[t : t + 1, g * HD : (g + 1) * HD].astype(jnp.float32)
            sums[g] = sums[g] + factor[:, g : g + 1] * value

    def add(d, state):
        norm, sums = state
        factor = jnp.exp(sbuf[d] - top)
        sums = tuple(
            sums[g] + factor[:, g : g + 1] * pbuf[d, g].astype(jnp.float32) for g in range(KVH)
        )
        return norm + factor, sums

    norm, sums = lax.fori_loop(0, depth, add, (norm, tuple(sums)))
    for g in range(KVH):
        result = (sums[g] / norm[:, g : g + 1]).astype(pre_out.dtype)
        for h in range(GROUP):
            at = (g * GROUP + h) * HD
            pre_out[0:1, at : at + HD] = result[h : h + 1]
            for s in range(STEPS):
                r = (s + 1) * GROUP + h
                dec_out[s : s + 1, at : at + HD] = result[r : r + 1]

    if split:
        each(groups, my_g, lambda g: share(g, True).wait_recv())
        tables = pltpu.make_async_copy(meta_x, meta_xs, local.at[9])
        tables.start()
        tables.wait()

        def worst(i, sofar):
            return jnp.maximum(sofar, meta_s[i, ROUTE, 4 * cap + 1])

        over = lax.fori_loop(0, n, worst, jnp.int32(0))
        for other_g in range(groups):
            def worse(i, sofar):
                return jnp.maximum(
                    sofar, jnp.where(my_g == other_g, 0, meta_xs[other_g, i, ROUTE, 4 * cap + 1])
                )

            over = lax.fori_loop(0, n, worse, over)
        flag_out[0] = over

        @pl.when(inner)
        def _():
            for piece in keys_at:
                unpack(piece, INNER, True)
            pass_on(values_at, OUTER)
            for piece in keys_at:
                unpack(piece, OUTER, True)
            for piece in values_at:
                unpack(piece, OUTER, True)
            for piece in values_at:
                unpack(piece, INNER, True)

        @pl.when(jnp.logical_not(inner))
        def _():
            for numbers in (keys_at, values_at):
                for side in (INNER, OUTER):
                    for piece in numbers:
                        unpack(piece, side, False)

    pair(0, q_y_out, q_y_out, across).wait_send()
    pair(1, q_c_out, q_c_out, sibling).wait_send()
    for copy in (part1, part1s, part2, part2s):
        copy.wait_send()

    def finish_row(z):
        for kind in (QROW, PART, STAT):
            row(kind, z).wait_send()

    each(depth, my_z, finish_row)
    own_page(KEYS).wait()
    own_page(VALUES).wait()
    each(n, me, lambda peer: page(META, peer).wait_send())

    def finish(peer):
        page(KEYS, peer, True).wait_recv()
        page(VALUES, peer, True).wait_recv()
        for kind in (KEYS, VALUES):
            page(kind, peer).wait_send()

    if split:
        each(groups, my_g, lambda g: share(g).wait_send())
        each(n // 2, me - base, lambda i: finish(base + i))
        for item in order:
            cross(*item, INNER).wait_send()
        for piece in range(2 * parts):
            @pl.when(inner)
            def _():
                for side in (INNER, OUTER):
                    hand(piece, side).wait_send()

            for zi in range(2):
                def settle(to):
                    fan(piece, zi, to, plane).wait_send()
                    fan(piece, zi, to, to).wait_recv()

                each(4, plane, settle)
    else:
        each(n, me, finish)


def main(n, cap, split, groups, counts, q, meta, ck, cv, pk, pv, own_k, own_v, cross):
    height = n * ROWS
    chunk = min(height, 384)
    _, dense, tail = plan(n, cap)
    parts_count = 2
    vmem = pl.BlockSpec(memory_space=pltpu.VMEM)
    smem = pl.BlockSpec(memory_space=pltpu.SMEM)
    hbm = pl.BlockSpec(memory_space=pltpu.HBM)

    def parts(rows):
        return pltpu.VMEM((KVH, rows, HD), jnp.bfloat16)

    def stats(rows):
        return pltpu.VMEM((rows, LANES), jnp.float32)

    half, quarter, depth = height // 2, height // 4, n // 4
    store = (n * cap, PAGE, KVD)
    out_shape = [
        jax.ShapeDtypeStruct((1, HQ * HD), q.dtype),
        jax.ShapeDtypeStruct((STEPS, HQ * HD), q.dtype),
        jax.ShapeDtypeStruct(store, pk.dtype),
        jax.ShapeDtypeStruct(store, pv.dtype),
        jax.ShapeDtypeStruct(meta.shape, meta.dtype),
    ]
    out_specs = [vmem] * 5
    scratch = [
        pltpu.VMEM(ck.shape, ck.dtype), pltpu.VMEM(cv.shape, cv.dtype),
        pltpu.SMEM(meta.shape, jnp.int32),
        parts(height), parts(height), stats(height), pltpu.VMEM((height, LANES), jnp.int32),
        parts(half), stats(half), parts(half), stats(half),
        parts(quarter), stats(quarter), parts(quarter), stats(quarter),
        pltpu.VMEM((depth, KVH, ROWS, HD), jnp.bfloat16),
        pltpu.VMEM((depth, ROWS, LANES), jnp.float32),
        pltpu.SemaphoreType.DMA((3, n)),
        pltpu.SemaphoreType.DMA((3, n)),
        pltpu.SemaphoreType.DMA((3, depth)),
        pltpu.SemaphoreType.DMA((3, depth)),
        pltpu.SemaphoreType.DMA((6,)),
        pltpu.SemaphoreType.DMA((6,)),
        pltpu.SemaphoreType.DMA((10,)),
    ]
    if split:
        out_shape.append(jax.ShapeDtypeStruct((1,), jnp.int32))
        out_specs.append(smem)
        count = 2 * parts_count
        scratch += [
            pltpu.VMEM((groups,) + meta.shape, jnp.int32),
            pltpu.SMEM((groups,) + meta.shape, jnp.int32),
            *[pltpu.VMEM((dense, PAGE, w), pk.dtype) for _, _, w in pieces_of(parts_count) * 2],
            pltpu.VMEM((2, 4, cap, PAGE, KVD), pk.dtype),
            pltpu.VMEM((2, 4, cap, PAGE, KVD), pv.dtype),
            pltpu.SemaphoreType.DMA((groups,)),
            pltpu.SemaphoreType.DMA((groups,)),
            pltpu.SemaphoreType.DMA((count, 2)),
            pltpu.SemaphoreType.DMA((count, 2, 2)),
            pltpu.SemaphoreType.DMA((count, 2)),
            pltpu.SemaphoreType.DMA((count, 2)),
            pltpu.SemaphoreType.DMA((count, 2, 4)),
            pltpu.SemaphoreType.DMA((count, 2, 4)),
        ]
    return pl.pallas_call(
        functools.partial(main_kernel, n, cap, chunk, split, dense, tail, parts_count),
        in_specs=[smem] + [vmem] * 2 + [hbm] * 2 + [vmem] * (4 + len(cross)),
        out_specs=out_specs,
        out_shape=out_shape,
        scratch_shapes=scratch,
        compiler_params=pltpu.CompilerParams(
            collective_id=0, has_side_effects=True, vmem_limit_bytes=32 << 20
        ),
        name="exchange",
    )(counts, q, meta, ck, cv, pk, pv, own_k, own_v, *cross)


def direct_kernel(n, cap, pk_ref, pv_ref, store_k, store_v, send, recv, local):
    me = lax.axis_index("seq")

    def slots_of(d):
        return pl.ds(d * cap, cap)

    def ends(kind, to, writer):
        src, dst = (pk_ref, store_k) if kind == 0 else (pv_ref, store_v)
        return src.at[slots_of(to)], dst.at[slots_of(writer)]

    def page(kind, peer, arriving=False):
        src, dst = ends(kind, peer, peer if arriving else me)
        return pltpu.make_async_remote_copy(
            src_ref=src, dst_ref=dst, send_sem=send.at[kind, peer],
            recv_sem=recv.at[kind, peer if arriving else me],
            device_id={"seq": peer}, device_id_type=MESH,
        )

    def each(body):
        def step(i, _):
            body(lax.rem(me + i, n))
            return 0

        lax.fori_loop(1, n, step, 0)

    barrier = pltpu.get_barrier_semaphore()
    each(
        lambda peer: pl.semaphore_signal(
            barrier, inc=1, device_id={"seq": peer}, device_id_type=MESH
        )
    )
    pl.semaphore_wait(barrier, n - 1)
    own = []
    for kind in range(2):
        each(lambda peer: page(kind, peer).start())
        src, dst = ends(kind, me, me)
        own.append(pltpu.make_async_copy(src, dst, local.at[kind]))
        own[-1].start()
    for kind in range(2):
        own[kind].wait()
        each(lambda peer: page(kind, peer, True).wait_recv())
        each(lambda peer: page(kind, peer).wait_send())


def direct(n, cap, pk, pv):
    vmem = pl.BlockSpec(memory_space=pltpu.VMEM)
    return pl.pallas_call(
        functools.partial(direct_kernel, n, cap),
        in_specs=[vmem] * 2,
        out_specs=[vmem] * 2,
        out_shape=[jax.ShapeDtypeStruct(x.shape, x.dtype) for x in (pk, pv)],
        scratch_shapes=[
            pltpu.SemaphoreType.DMA((2, n)),
            pltpu.SemaphoreType.DMA((2, n)),
            pltpu.SemaphoreType.DMA((2,)),
        ],
        compiler_params=pltpu.CompilerParams(
            collective_id=1, has_side_effects=True, vmem_limit_bytes=16 << 20
        ),
        name="direct",
    )(pk, pv)


def write_kernel(
    n, cap, k_in, v_in, pre_in, dec_in, meta_in,
    k_out, v_out, pre_out, dec_out, ids_out, ids, done,
):
    copies = [
        pltpu.make_async_copy(k_in, k_out, done.at[0]),
        pltpu.make_async_copy(v_in, v_out, done.at[1]),
        pltpu.make_async_copy(pre_in, pre_out, done.at[2]),
        pltpu.make_async_copy(dec_in, dec_out, done.at[3]),
    ]
    for copy in copies:
        copy.start()
    lane = lax.broadcasted_iota(jnp.int32, (1, n * cap), 1)
    row = meta_in[0, IDS : IDS + 1, :]
    for s in range(1, n):
        row = jnp.where(lane // cap == s, meta_in[s, IDS : IDS + 1, :], row)
    ids[...] = row
    last = pltpu.make_async_copy(ids, ids_out, done.at[4])
    last.start()
    for copy in copies + [last]:
        copy.wait()


def write(n, cap, store_k, store_v, pre, dec, meta):
    vmem = pl.BlockSpec(memory_space=pltpu.VMEM)
    hbm = pl.BlockSpec(memory_space=pltpu.HBM)
    return pl.pallas_call(
        functools.partial(write_kernel, n, cap),
        in_specs=[vmem] * 5,
        out_specs=[hbm] * 5,
        out_shape=[jax.ShapeDtypeStruct(x.shape, x.dtype) for x in (store_k, store_v, pre, dec)]
        + [jax.ShapeDtypeStruct((1, n * cap), jnp.int32)],
        scratch_shapes=[pltpu.VMEM((1, n * cap), jnp.int32), pltpu.SemaphoreType.DMA((5,))],
        compiler_params=pltpu.CompilerParams(vmem_limit_bytes=16 << 20),
        name="write",
    )(store_k, store_v, pre, dec, meta)


def per_device(
    prefill_q, cache_k, cache_v, page_counts, page_owner, decode_q, decode_k, decode_v, context_len
):
    n = lax.axis_size("seq")
    groups = lax.axis_size("groups")
    page_slots = cache_k.shape[0] // PAGE
    cap = max(2, 2 * page_slots // n)
    split, _, _ = plan(n, cap)
    ck = cache_k.reshape(page_slots, PAGE, KVD)
    cv = cache_v.reshape(page_slots, PAGE, KVD)
    owner = page_owner[:, 0]
    parts = (page_counts, context_len, ck, cv, prefill_q, decode_q[0])
    pk, pv, *cross, q, meta = prep(n, cap, split, owner, *parts)
    pre, dec, store_k, store_v, meta, *flag = main(
        n, cap, split, groups, page_counts, q, meta, cache_k, cache_v, pk, pv,
        decode_k[0], decode_v[0], cross,
    )

    def keep(sk, sv, pre, dec, meta):
        return write(n, cap, sk, sv, pre, dec, meta)

    def again(sk, sv, pre, dec, meta):
        pk, pv, _, _ = prep(n, cap, False, owner, *parts)
        sk, sv = direct(n, cap, pk, pv)
        return write(n, cap, sk, sv, pre, dec, meta)

    if split:
        results = lax.cond(flag[0][0] > 0, again, keep, store_k, store_v, pre, dec, meta)
    else:
        results = keep(store_k, store_v, pre, dec, meta)
    store_k, store_v, pre, dec, ids = results
    return (
        pre,
        dec.reshape(1, STEPS, HQ * HD),
        store_k.reshape(-1, KVD),
        store_v.reshape(-1, KVD),
        ids.reshape(-1),
    )


def solution(mesh):
    both = ("groups", "seq")
    in_specs = (
        P(both, None),
        P(both, None),
        P(both, None),
        P("groups"),
        P(both, None),
        P(both, None, None),
        P(both, None, None),
        P(both, None, None),
        P(both),
    )
    out_specs = (
        P(both, None),
        P(both, None, None),
        P(both, None),
        P(both, None),
        P(both),
    )
    return jax.shard_map(
        per_device, mesh=mesh, in_specs=in_specs, out_specs=out_specs, check_vma=False
    )
```

```python
import functools

import jax
import jax.numpy as jnp
from jax import lax
from jax.experimental import pallas as pl
from jax.experimental.pallas import tpu as pltpu
from jax.sharding import PartitionSpec as P

HQ = 64
KVH = 8
HD = 128
PAGE = 8
STEPS = 2
KVD = 1024
GROUP = HQ // KVH
ROWS = (1 + STEPS) * GROUP
LANES = 128
MASKED = -1e30
SCALE = HD ** (-0.5)
MESH = pl.DeviceIdType.MESH

META, KEYS, VALUES = range(3)
QROW, PART, STAT = range(3)
IDS, ROUTE = range(2)


def plan(n, cap):
    if n // 4 != 4 or n % 4:
        return False, 0, 0
    most = cap * n // 2
    return True, most * 11 // 16, most // 2 * 7 // 8


def pieces_of(parts):
    width = KVD // parts
    return [(kind, i * width, width) for kind in (KEYS, VALUES) for i in range(parts)]


def prep_kernel(
    n, cap, page_slots, split, dense, tail,
    owner, counts, context, ck_hbm, cv_hbm, pq, dq,
    out_k, out_v, *rest,
):
    if split:
        cross_k, cross_v, q_out, meta, ck, cv, table, seen, cross, tally, done = rest
    else:
        q_out, meta, ck, cv, table, seen, done = rest
    me = lax.axis_index("seq")
    my_z, plane = me // 4, me % 4
    half = my_z // 2
    span = n // 2 if split else n
    base = half * span if split else 0
    loads = [
        pltpu.make_async_copy(ck_hbm, ck, done.at[0]),
        pltpu.make_async_copy(cv_hbm, cv, done.at[1]),
    ]
    for load in loads:
        load.start()

    for s in range(1 + STEPS):
        for h in range(HQ):
            row = s * GROUP + h % GROUP
            src = pq if s == 0 else dq
            at = 0 if s == 0 else s - 1
            q_out[h // GROUP, row : row + 1, :] = src[at : at + 1, h * HD : (h + 1) * HD]

    def clear(i, _):
        seen[i] = 0
        for k in range(cap):
            table[i * cap + k] = -1
            meta[i, IDS, me * cap + k] = -1
        meta[i, ROUTE, 4 * cap] = context[0]
        return 0

    lax.fori_loop(0, n, clear, 0)
    if split:
        near = (2 - half) * 4 + plane
        far = 3 * (1 - half) * 4 + plane
        for k in range(4 * cap):
            meta[near, ROUTE, k] = -1
            meta[far, ROUTE, k] = -1

        def zero(i, _):
            cross[i] = 0
            return 0

        lax.fori_loop(0, dense, zero, 0)
        tally[0] = 0
        tally[1] = 0
        tally[2] = 0

    def place(j, _):
        o = owner[j]
        k = seen[o]
        seen[o] = k + 1
        table[o * cap + k] = j
        meta[o, IDS, me * cap + k] = me * page_slots + j
        if split:
            @pl.when(o // 4 // 2 != half)
            def _():
                front, back = tally[0], tally[1]
                room = front + back < dense
                at = (o % 4) * cap + k

                @pl.when(room & (o // 4 == 2 - half))
                def _():
                    cross[front] = j
                    meta[near, ROUTE, at] = front
                    tally[0] = front + 1

                fits = room & (back < tail)

                @pl.when(fits & (o // 4 != 2 - half))
                def _():
                    cross[dense - 1 - back] = j
                    meta[far, ROUTE, at] = tail - 1 - back
                    tally[1] = back + 1

                @pl.when(jnp.logical_not(jnp.where(o // 4 == 2 - half, room, fits)))
                def _():
                    tally[2] = 1

        return 0

    lax.fori_loop(0, counts[me], place, 0)

    if split:
        def flag(i, _):
            meta[i, ROUTE, 4 * cap + 1] = tally[2]
            return 0

        lax.fori_loop(0, n, flag, 0)

    for load in loads:
        load.wait()

    if split:
        def pick(i, _):
            page = cross[i]
            cross_k[i] = ck[page]
            cross_v[i] = cv[page]
            return 0

        lax.fori_loop(0, dense, pick, 0)

    def fill(i, _):
        for k in range(cap):
            src = table[(base + i) * cap + k]
            page = jnp.maximum(src, 0)
            there = jnp.full((PAGE, KVD), src, jnp.int32) >= 0
            out_k[i * cap + k] = jnp.where(there, ck[page], jnp.zeros((), out_k.dtype))
            out_v[i * cap + k] = jnp.where(there, cv[page], jnp.zeros((), out_v.dtype))
        return 0

    lax.fori_loop(0, span, fill, 0)


def prep(n, cap, split, owner, counts, context, ck, cv, pq, dq):
    page_slots = ck.shape[0]
    _, dense, tail = plan(n, cap)
    smem = pl.BlockSpec(memory_space=pltpu.SMEM)
    vmem = pl.BlockSpec(memory_space=pltpu.VMEM)
    hbm = pl.BlockSpec(memory_space=pltpu.HBM)
    span = n // 2 if split else n

    def pages(count):
        return [jax.ShapeDtypeStruct((count, PAGE, KVD), x.dtype) for x in (ck, cv)]

    out_shape = pages(span * cap) + (pages(dense) if split else [])
    out_specs = [vmem] * len(out_shape) + [vmem, smem]
    out_shape += [
        jax.ShapeDtypeStruct((KVH, ROWS, HD), pq.dtype),
        jax.ShapeDtypeStruct((n, 2, n * cap), jnp.int32),
    ]
    scratch = [
        pltpu.VMEM(ck.shape, ck.dtype), pltpu.VMEM(cv.shape, cv.dtype),
        pltpu.SMEM((n * cap,), jnp.int32), pltpu.SMEM((n,), jnp.int32),
    ]
    if split:
        scratch += [pltpu.SMEM((dense,), jnp.int32), pltpu.SMEM((4,), jnp.int32)]
    return pl.pallas_call(
        functools.partial(prep_kernel, n, cap, page_slots, split, dense, tail),
        in_specs=[smem, smem, smem, hbm, hbm, vmem, vmem],
        out_specs=out_specs,
        out_shape=out_shape,
        scratch_shapes=scratch + [pltpu.SemaphoreType.DMA((2,))],
        compiler_params=pltpu.CompilerParams(vmem_limit_bytes=16 << 20),
        name="prep",
    )(owner, counts, context, ck, cv, pq, dq)


def main_kernel(
    n, cap, chunk, split, dense, tail, parts,
    counts, q_ref, meta_ref, ck_hbm, cv_hbm, pk_ref, pv_ref, ok_ref, ov_ref, *rest,
):
    if split:
        mk_ref, mv_ref = rest[:2]
        rest = rest[2:]
    pre_out, dec_out, store_k, store_v, meta_out = rest[:5]
    rest = rest[5:]
    if split:
        flag_out = rest[0]
        rest = rest[1:]
    (
        ck_ref, cv_ref, meta_s,
        qbuf, obuf, stat, limit, got1, got1s, obuf1, stat1, got2, got2s, obuf2, stat2, pbuf, sbuf,
        page_send, page_recv, row_send, row_recv, pair_send, pair_recv, local,
    ) = rest[:24]
    rest = rest[24:]
    if split:
        (
            meta_x, meta_xs, *lands, fan_k, fan_v,
            x_send, x_recv, cross_send, cross_recv, pass_send, pass_recv, fan_send, fan_recv,
        ) = rest
    depth = n // 4
    groups = lax.axis_size("groups")
    my_g = lax.axis_index("groups")
    me = lax.axis_index("seq")
    my_z, my_y, my_c = me // 4, (me // 2) % 2, me % 2
    plane = me % 4
    half = my_z // 2
    across = my_z * 4 + (1 - my_y) * 2 + my_c
    sibling = my_z * 4 + my_y * 2 + (1 - my_c)
    base = half * (n // 2) if split else 0

    def rows_of(first, count=1):
        return pl.ds(pl.multiple_of(first * ROWS, 8), count * ROWS)

    def slots_of(d):
        return pl.ds(d * cap, cap)

    def page_ends(kind, peer, writer):
        if kind == META:
            return meta_ref.at[peer], meta_out.at[writer]
        if kind == KEYS:
            return pk_ref.at[slots_of(peer - base)], store_k.at[slots_of(writer)]
        return pv_ref.at[slots_of(peer - base)], store_v.at[slots_of(writer)]

    def page(kind, peer, arriving=False):
        src, dst = page_ends(kind, me if arriving else peer, peer if arriving else me)
        return pltpu.make_async_remote_copy(
            src_ref=src, dst_ref=dst, send_sem=page_send.at[kind, peer],
            recv_sem=page_recv.at[kind, peer if arriving else me],
            device_id={"seq": peer}, device_id_type=MESH,
        )

    def row_ends(kind, z, writer):
        if kind == QROW:
            return q_ref, qbuf.at[:, rows_of((my_c * 2 + my_y) * depth + writer), :]
        if kind == PART:
            return obuf2.at[:, rows_of(z), :], pbuf.at[writer]
        return stat2.at[rows_of(z), :], sbuf.at[writer]

    def row(kind, z, arriving=False):
        src, dst = row_ends(kind, z, z if arriving else my_z)
        return pltpu.make_async_remote_copy(
            src_ref=src, dst_ref=dst, send_sem=row_send.at[kind, z],
            recv_sem=row_recv.at[kind, z if arriving else my_z],
            device_id={"seq": z * 4 + my_y * 2 + my_c}, device_id_type=MESH,
        )

    def pair(number, src, dst, peer):
        return pltpu.make_async_remote_copy(
            src_ref=src, dst_ref=dst, send_sem=pair_send.at[number], recv_sem=pair_recv.at[number],
            device_id={"seq": peer}, device_id_type=MESH,
        )

    def own_page(kind):
        src, dst = page_ends(kind, me, me)
        return pltpu.make_async_copy(src, dst, local.at[kind])

    def own_row(kind):
        src, dst = row_ends(kind, my_z, my_z)
        return pltpu.make_async_copy(src, dst, local.at[3 + kind])

    def each(count, mine, body):
        def step(i, _):
            body(lax.rem(mine + i, count))
            return 0

        lax.fori_loop(1, count, step, 0)

    caches = [
        pltpu.make_async_copy(ck_hbm, ck_ref, local.at[6]),
        pltpu.make_async_copy(cv_hbm, cv_ref, local.at[7]),
    ]
    for load in caches:
        load.start()

    barrier = pltpu.get_barrier_semaphore()

    def greet(peer):
        pl.semaphore_signal(barrier, inc=1, device_id={"seq": peer}, device_id_type=MESH)

    def greet_group(g):
        pl.semaphore_signal(barrier, inc=1, device_id={"groups": g}, device_id_type=MESH)

    each(n, me, greet)
    if split:
        each(groups, my_g, greet_group)
    pl.semaphore_wait(barrier, n - 1 + (groups - 1 if split else 0))

    if split:
        pieces = pieces_of(parts)
        inner = my_z == 1 + half
        other = (1 - half) * 2
        by_inner, by_outer = half, 1 - half
        keys_at, values_at = range(parts), range(parts, 2 * parts)
        HEAD, TAIL = 0, 1
        INNER, OUTER = 0, 1
        lands = lands[: len(pieces)], lands[len(pieces) :]
        spans = (pl.ds(0, dense - tail), pl.ds(dense - tail, tail))

        def cross(piece, end, side):
            kind, col, width = pieces[piece]
            src = mk_ref if kind == KEYS else mv_ref
            return pltpu.make_async_remote_copy(
                src_ref=src.at[spans[end], :, pl.ds(col, width)],
                dst_ref=lands[side][piece].at[spans[end]],
                send_sem=cross_send.at[piece, end], recv_sem=cross_recv.at[piece, end, side],
                device_id={"seq": (2 - half) * 4 + plane}, device_id_type=MESH,
            )

        def hand(piece, side):
            buf = lands[side][piece]
            return pltpu.make_async_remote_copy(
                src_ref=buf.at[spans[TAIL]], dst_ref=buf.at[pl.ds(0, tail)],
                send_sem=pass_send.at[piece, side], recv_sem=pass_recv.at[piece, side],
                device_id={"seq": 3 * half * 4 + plane}, device_id_type=MESH,
            )

        def fan(piece, zi, to, writer):
            kind, col, width = pieces[piece]
            src = fan_k if kind == KEYS else fan_v
            dst = store_k if kind == KEYS else store_v
            cols = pl.ds(col, width)
            shard = (other + zi) * 4 + writer
            return pltpu.make_async_remote_copy(
                src_ref=src.at[zi, to, :, :, cols], dst_ref=dst.at[slots_of(shard), :, cols],
                send_sem=fan_send.at[piece, zi, to], recv_sem=fan_recv.at[piece, zi, writer],
                device_id={"seq": my_z * 4 + to}, device_id_type=MESH,
            )

        def launch(items, side):
            for item in items:
                cross(*item, side).start()

        def pass_on(numbers, side):
            @pl.when(inner)
            def _():
                for piece in numbers:
                    cross(piece, TAIL, side).wait_recv()
                    hand(piece, side).start()

        def unpack(piece, side, near):
            kind, col, width = pieces[piece]
            buf = lands[side][piece]
            out = fan_k if kind == KEYS else fan_v
            keep = store_k if kind == KEYS else store_v
            cols = pl.ds(col, width)
            if near:
                cross(piece, HEAD, side).wait_recv()
            else:
                hand(piece, side).wait_recv()
            zi = by_inner if side == INNER else by_outer
            shard = (other + zi) * 4 + plane

            def page_at(to, k):
                at = meta_s[shard, ROUTE, to * cap + k]
                there = jnp.full((PAGE, width), at, jnp.int32) >= 0
                return jnp.where(there, buf[jnp.maximum(at, 0)], jnp.zeros((), buf.dtype))

            def send(to):
                for k in range(cap):
                    out[zi, to, k, :, cols] = page_at(to, k)
                fan(piece, zi, to, plane).start()

            each(4, plane, send)
            for k in range(cap):
                keep[shard * cap + k, :, cols] = page_at(plane, k)

    each(depth, my_z, lambda z: row(QROW, z).start())
    own_row(QROW).start()
    each(n, me, lambda peer: page(META, peer).start())
    for kind in (META, KEYS, VALUES):
        own_page(kind).start()

    if split:
        order = [(p, TAIL) for p in range(2 * parts)] + [(p, HEAD) for p in range(2 * parts)]

        @pl.when(inner)
        def _():
            launch(order[:-parts], INNER)

    def start_pages(peer):
        page(KEYS, peer).start()
        page(VALUES, peer).start()

    own_row(QROW).wait()
    each(depth, my_z, lambda z: row(QROW, z, True).wait_recv())
    own_page(META).wait()
    each(n, me, lambda peer: page(META, peer, True).wait_recv())
    if split:
        first = half * 2
        other_z = first + (1 - my_z % 2)
        @pl.when(jnp.logical_not(inner))
        def _():
            launch(order[:parts], OUTER)

        start_pages(other_z * 4 + plane)
        start_pages(other_z * 4 + my_y * 2 + (1 - my_c))
    else:
        def near(i, _):
            z = lax.rem(my_z + depth // 2 + i, depth)

            @pl.when(z != my_z)
            def _():
                start_pages(z * 4 + my_y * 2 + my_c)
                start_pages(z * 4 + my_y * 2 + (1 - my_c))

            return 0

        lax.fori_loop(0, depth, near, 0)

    q_y_out = qbuf.at[:, rows_of((my_c * 2 + my_y) * depth, depth), :]
    q_y_in = qbuf.at[:, rows_of((my_c * 2 + 1 - my_y) * depth, depth), :]
    pair(0, q_y_out, q_y_out, across).start()
    if split:
        start_pages(my_z * 4 + (1 - my_y) * 2 + my_c)
        start_pages(my_z * 4 + (1 - my_y) * 2 + (1 - my_c))
    pair(0, q_y_out, q_y_in, across).wait_recv()
    q_c_out = qbuf.at[:, rows_of(my_c * 2 * depth, 2 * depth), :]
    q_c_in = qbuf.at[:, rows_of((1 - my_c) * 2 * depth, 2 * depth), :]
    pair(1, q_c_out, q_c_out, sibling).start()
    table = pltpu.make_async_copy(meta_out, meta_s, local.at[8])
    table.start()
    if split:
        def share(g, arriving=False):
            return pltpu.make_async_remote_copy(
                src_ref=meta_out, dst_ref=meta_x.at[g if arriving else my_g],
                send_sem=x_send.at[g], recv_sem=x_recv.at[g if arriving else my_g],
                device_id={"groups": g}, device_id_type=MESH,
            )

        each(groups, my_g, lambda g: share(g).start())
    table.wait()

    live = PAGE * counts[me]
    start = PAGE * lax.fori_loop(
        0, n, lambda i, sofar: sofar + jnp.where(i < me, counts[i], 0), jnp.int32(0)
    )
    prompt = PAGE * lax.fori_loop(0, n, lambda i, sofar: sofar + counts[i], jnp.int32(0))

    def set_limit(p, _):
        d = (p % depth) * 4 + ((p // depth) % 2) * 2 + p // (2 * depth)
        at = pl.multiple_of(p * ROWS, 8)
        reach = jnp.minimum(live, meta_s[d, ROUTE, 4 * cap] - start)
        limit[pl.ds(at, 8), :] = jnp.full(
            (8, LANES), jnp.minimum(live, prompt - n + d + 1 - start)
        )
        for s in range(STEPS):
            limit[pl.ds(pl.multiple_of(at + 8 * (s + 1), 8), 8), :] = jnp.full((8, LANES), reach)
        return 0

    lax.fori_loop(0, n, set_limit, 0)
    pair(1, q_c_out, q_c_in, sibling).wait_recv()
    for load in caches:
        load.wait()

    def far(i, _):
        z = lax.rem(my_z + depth // 2 + i, depth)
        start_pages(z * 4 + (1 - my_y) * 2 + my_c)
        start_pages(z * 4 + (1 - my_y) * 2 + (1 - my_c))
        return 0

    if not split:
        far(0, 0)

    lane = lax.broadcasted_iota(jnp.int32, (chunk, LANES), 1)
    keys = ck_ref.shape[0]

    def attend(c, _):
        rows = pl.ds(pl.multiple_of(c * chunk, 16), chunk)

        def head(g, stats):
            cols = pl.ds(pl.multiple_of(g * HD, HD), HD)
            scores = lax.dot_general(
                qbuf[g, rows, :], ck_ref[:, cols], (((1,), (1,)), ((), ())),
                preferred_element_type=jnp.float32,
            ) * SCALE
            place = lax.broadcasted_iota(jnp.int32, (chunk, keys), 1)
            bound = limit[rows, 0:1]
            scores = jnp.where(place < bound, scores, MASKED)
            high = jnp.max(scores, axis=1, keepdims=True)
            weights = jnp.exp(scores - high)
            total = jnp.sum(weights, axis=1, keepdims=True)
            summed = jnp.dot(
                weights.astype(jnp.bfloat16), cv_ref[:, cols], preferred_element_type=jnp.float32
            )
            obuf[g, rows, :] = (summed / total).astype(jnp.bfloat16)
            level = jnp.where(bound > 0, high + jnp.log(total), MASKED)
            return jnp.where(lane == g, level, stats)

        stat[rows, :] = lax.fori_loop(0, KVH, head, jnp.zeros((chunk, LANES), jnp.float32))
        return 0

    lax.fori_loop(0, stat.shape[0] // chunk, attend, 0)

    def merge(a, a_stat, first, b, b_stat, to, to_stat):
        step = 2 * ROWS

        def some(i, _):
            here = pl.ds(pl.multiple_of(i * step, 16), step)
            there = pl.ds(pl.multiple_of(first * ROWS + i * step, 16), step)
            one, two = a_stat[there, :], b_stat[here, :]
            high = jnp.maximum(one, two)
            one, two = jnp.exp(one - high), jnp.exp(two - high)
            both = one + two
            to_stat[here, :] = high + jnp.log(both)
            one, two = one / both, two / both
            for g in range(KVH):
                to[g, here, :] = (
                    one[:, g : g + 1] * a[g, there, :].astype(jnp.float32)
                    + two[:, g : g + 1] * b[g, here, :].astype(jnp.float32)
                ).astype(jnp.bfloat16)
            return 0

        lax.fori_loop(0, to_stat.shape[0] // step, some, 0)

    give = (1 - my_c) * 2 * depth
    part1 = pair(2, obuf.at[:, rows_of(give, 2 * depth), :], got1, sibling)
    part1s = pair(3, stat.at[rows_of(give, 2 * depth), :], got1s, sibling)
    part1s.start()
    part1.start()
    if split:
        pass_on(keys_at, OUTER)
    part1s.wait_recv()
    part1.wait_recv()
    merge(obuf, stat, my_c * 2 * depth, got1, got1s, obuf1, stat1)
    give = (1 - my_y) * depth
    part2 = pair(4, obuf1.at[:, rows_of(give, depth), :], got2, across)
    part2s = pair(5, stat1.at[rows_of(give, depth), :], got2s, across)
    part2s.start()
    part2.start()
    start_pages(sibling)
    if split:
        pass_on(keys_at, INNER)

    own_lane = lax.broadcasted_iota(jnp.int32, (ROWS, LANES), 1)
    own_place = lax.broadcasted_iota(jnp.int32, (ROWS, LANES), 0)
    own_levels = []
    for t in range(STEPS):
        level = jnp.zeros((ROWS, LANES), jnp.float32)
        for g in range(KVH):
            key = ok_ref[t : t + 1, g * HD : (g + 1) * HD].astype(jnp.float32)
            score = jnp.sum(q_ref[g].astype(jnp.float32) * key, axis=1, keepdims=True) * SCALE
            level = jnp.where(own_lane == g, score, level)
        own_levels.append(jnp.where(own_place >= GROUP * (t + 1), level, MASKED))

    part2s.wait_recv()
    part2.wait_recv()
    merge(obuf1, stat1, my_y * depth, got2, got2s, obuf2, stat2)

    def start_rows(z):
        row(STAT, z).start()
        row(PART, z).start()

    each(depth, my_z, start_rows)
    own_row(STAT).start()
    own_row(PART).start()

    if split:
        @pl.when(inner)
        def _():
            launch(order[-parts:], INNER)

        start_pages(other_z * 4 + (1 - my_y) * 2 + my_c)
        start_pages(other_z * 4 + (1 - my_y) * 2 + (1 - my_c))
    else:
        lax.fori_loop(1, depth, far, 0)

    if split:
        pass_on(values_at, INNER)

    own_row(STAT).wait()
    own_row(PART).wait()

    def wait_rows(z):
        row(STAT, z, True).wait_recv()
        row(PART, z, True).wait_recv()

    each(depth, my_z, wait_rows)

    if split:
        @pl.when(jnp.logical_not(inner))
        def _():
            launch(order[parts:], OUTER)

    top = functools.reduce(jnp.maximum, own_levels)
    top = lax.fori_loop(0, depth, lambda d, high: jnp.maximum(high, sbuf[d]), top)

    norm = jnp.zeros((ROWS, LANES), jnp.float32)
    sums = [jnp.zeros((ROWS, HD), jnp.float32) for _ in range(KVH)]
    for t in range(STEPS):
        factor = jnp.exp(own_levels[t] - top)
        norm = norm + factor
        for g in range(KVH):
            value = ov_ref[t : t + 1, g * HD : (g + 1) * HD].astype(jnp.float32)
            sums[g] = sums[g] + factor[:, g : g + 1] * value

    def add(d, state):
        norm, sums = state
        factor = jnp.exp(sbuf[d] - top)
        sums = tuple(
            sums[g] + factor[:, g : g + 1] * pbuf[d, g].astype(jnp.float32) for g in range(KVH)
        )
        return norm + factor, sums

    norm, sums = lax.fori_loop(0, depth, add, (norm, tuple(sums)))
    for g in range(KVH):
        result = (sums[g] / norm[:, g : g + 1]).astype(pre_out.dtype)
        for h in range(GROUP):
            at = (g * GROUP + h) * HD
            pre_out[0:1, at : at + HD] = result[h : h + 1]
            for s in range(STEPS):
                r = (s + 1) * GROUP + h
                dec_out[s : s + 1, at : at + HD] = result[r : r + 1]

    if split:
        each(groups, my_g, lambda g: share(g, True).wait_recv())
        tables = pltpu.make_async_copy(meta_x, meta_xs, local.at[9])
        tables.start()
        tables.wait()

        def worst(i, sofar):
            return jnp.maximum(sofar, meta_s[i, ROUTE, 4 * cap + 1])

        over = lax.fori_loop(0, n, worst, jnp.int32(0))
        for other_g in range(groups):
            def worse(i, sofar):
                return jnp.maximum(
                    sofar, jnp.where(my_g == other_g, 0, meta_xs[other_g, i, ROUTE, 4 * cap + 1])
                )

            over = lax.fori_loop(0, n, worse, over)
        flag_out[0] = over

        @pl.when(inner)
        def _():
            for piece in keys_at:
                unpack(piece, INNER, True)
            pass_on(values_at, OUTER)
            for piece in keys_at:
                unpack(piece, OUTER, True)
            for piece in values_at:
                unpack(piece, OUTER, True)
            for piece in values_at:
                unpack(piece, INNER, True)

        @pl.when(jnp.logical_not(inner))
        def _():
            for numbers in (keys_at, values_at):
                for side in (INNER, OUTER):
                    for piece in numbers:
                        unpack(piece, side, False)

    pair(0, q_y_out, q_y_out, across).wait_send()
    pair(1, q_c_out, q_c_out, sibling).wait_send()
    for copy in (part1, part1s, part2, part2s):
        copy.wait_send()

    def finish_row(z):
        for kind in (QROW, PART, STAT):
            row(kind, z).wait_send()

    each(depth, my_z, finish_row)
    own_page(KEYS).wait()
    own_page(VALUES).wait()
    each(n, me, lambda peer: page(META, peer).wait_send())

    def finish(peer):
        page(KEYS, peer, True).wait_recv()
        page(VALUES, peer, True).wait_recv()
        for kind in (KEYS, VALUES):
            page(kind, peer).wait_send()

    if split:
        each(groups, my_g, lambda g: share(g).wait_send())
        each(n // 2, me - base, lambda i: finish(base + i))
        for item in order:
            cross(*item, INNER).wait_send()
        for piece in range(2 * parts):
            @pl.when(inner)
            def _():
                for side in (INNER, OUTER):
                    hand(piece, side).wait_send()

            for zi in range(2):
                def settle(to):
                    fan(piece, zi, to, plane).wait_send()
                    fan(piece, zi, to, to).wait_recv()

                each(4, plane, settle)
    else:
        each(n, me, finish)


def main(n, cap, split, groups, counts, q, meta, ck, cv, pk, pv, own_k, own_v, cross):
    height = n * ROWS
    chunk = min(height, 384)
    _, dense, tail = plan(n, cap)
    parts_count = 2
    vmem = pl.BlockSpec(memory_space=pltpu.VMEM)
    smem = pl.BlockSpec(memory_space=pltpu.SMEM)
    hbm = pl.BlockSpec(memory_space=pltpu.HBM)

    def parts(rows):
        return pltpu.VMEM((KVH, rows, HD), jnp.bfloat16)

    def stats(rows):
        return pltpu.VMEM((rows, LANES), jnp.float32)

    half, quarter, depth = height // 2, height // 4, n // 4
    store = (n * cap, PAGE, KVD)
    out_shape = [
        jax.ShapeDtypeStruct((1, HQ * HD), q.dtype),
        jax.ShapeDtypeStruct((STEPS, HQ * HD), q.dtype),
        jax.ShapeDtypeStruct(store, pk.dtype),
        jax.ShapeDtypeStruct(store, pv.dtype),
        jax.ShapeDtypeStruct(meta.shape, meta.dtype),
    ]
    out_specs = [vmem] * 5
    scratch = [
        pltpu.VMEM(ck.shape, ck.dtype), pltpu.VMEM(cv.shape, cv.dtype),
        pltpu.SMEM(meta.shape, jnp.int32),
        parts(height), parts(height), stats(height), pltpu.VMEM((height, LANES), jnp.int32),
        parts(half), stats(half), parts(half), stats(half),
        parts(quarter), stats(quarter), parts(quarter), stats(quarter),
        pltpu.VMEM((depth, KVH, ROWS, HD), jnp.bfloat16),
        pltpu.VMEM((depth, ROWS, LANES), jnp.float32),
        pltpu.SemaphoreType.DMA((3, n)),
        pltpu.SemaphoreType.DMA((3, n)),
        pltpu.SemaphoreType.DMA((3, depth)),
        pltpu.SemaphoreType.DMA((3, depth)),
        pltpu.SemaphoreType.DMA((6,)),
        pltpu.SemaphoreType.DMA((6,)),
        pltpu.SemaphoreType.DMA((10,)),
    ]
    if split:
        out_shape.append(jax.ShapeDtypeStruct((1,), jnp.int32))
        out_specs.append(smem)
        count = 2 * parts_count
        scratch += [
            pltpu.VMEM((groups,) + meta.shape, jnp.int32),
            pltpu.SMEM((groups,) + meta.shape, jnp.int32),
            *[pltpu.VMEM((dense, PAGE, w), pk.dtype) for _, _, w in pieces_of(parts_count) * 2],
            pltpu.VMEM((2, 4, cap, PAGE, KVD), pk.dtype),
            pltpu.VMEM((2, 4, cap, PAGE, KVD), pv.dtype),
            pltpu.SemaphoreType.DMA((groups,)),
            pltpu.SemaphoreType.DMA((groups,)),
            pltpu.SemaphoreType.DMA((count, 2)),
            pltpu.SemaphoreType.DMA((count, 2, 2)),
            pltpu.SemaphoreType.DMA((count, 2)),
            pltpu.SemaphoreType.DMA((count, 2)),
            pltpu.SemaphoreType.DMA((count, 2, 4)),
            pltpu.SemaphoreType.DMA((count, 2, 4)),
        ]
    return pl.pallas_call(
        functools.partial(main_kernel, n, cap, chunk, split, dense, tail, parts_count),
        in_specs=[smem] + [vmem] * 2 + [hbm] * 2 + [vmem] * (4 + len(cross)),
        out_specs=out_specs,
        out_shape=out_shape,
        scratch_shapes=scratch,
        compiler_params=pltpu.CompilerParams(
            collective_id=0, has_side_effects=True, vmem_limit_bytes=32 << 20
        ),
        name="exchange",
    )(counts, q, meta, ck, cv, pk, pv, own_k, own_v, *cross)


def direct_kernel(n, cap, pk_ref, pv_ref, store_k, store_v, send, recv, local):
    me = lax.axis_index("seq")

    def slots_of(d):
        return pl.ds(d * cap, cap)

    def ends(kind, to, writer):
        src, dst = (pk_ref, store_k) if kind == 0 else (pv_ref, store_v)
        return src.at[slots_of(to)], dst.at[slots_of(writer)]

    def page(kind, peer, arriving=False):
        src, dst = ends(kind, peer, peer if arriving else me)
        return pltpu.make_async_remote_copy(
            src_ref=src, dst_ref=dst, send_sem=send.at[kind, peer],
            recv_sem=recv.at[kind, peer if arriving else me],
            device_id={"seq": peer}, device_id_type=MESH,
        )

    def each(body):
        def step(i, _):
            body(lax.rem(me + i, n))
            return 0

        lax.fori_loop(1, n, step, 0)

    barrier = pltpu.get_barrier_semaphore()
    each(
        lambda peer: pl.semaphore_signal(
            barrier, inc=1, device_id={"seq": peer}, device_id_type=MESH
        )
    )
    pl.semaphore_wait(barrier, n - 1)
    own = []
    for kind in range(2):
        each(lambda peer: page(kind, peer).start())
        src, dst = ends(kind, me, me)
        own.append(pltpu.make_async_copy(src, dst, local.at[kind]))
        own[-1].start()
    for kind in range(2):
        own[kind].wait()
        each(lambda peer: page(kind, peer, True).wait_recv())
        each(lambda peer: page(kind, peer).wait_send())


def direct(n, cap, pk, pv):
    vmem = pl.BlockSpec(memory_space=pltpu.VMEM)
    return pl.pallas_call(
        functools.partial(direct_kernel, n, cap),
        in_specs=[vmem] * 2,
        out_specs=[vmem] * 2,
        out_shape=[jax.ShapeDtypeStruct(x.shape, x.dtype) for x in (pk, pv)],
        scratch_shapes=[
            pltpu.SemaphoreType.DMA((2, n)),
            pltpu.SemaphoreType.DMA((2, n)),
            pltpu.SemaphoreType.DMA((2,)),
        ],
        compiler_params=pltpu.CompilerParams(
            collective_id=1, has_side_effects=True, vmem_limit_bytes=16 << 20
        ),
        name="direct",
    )(pk, pv)


def write_kernel(
    n, cap, k_in, v_in, pre_in, dec_in, meta_in,
    k_out, v_out, pre_out, dec_out, ids_out, ids, done,
):
    copies = [
        pltpu.make_async_copy(k_in, k_out, done.at[0]),
        pltpu.make_async_copy(v_in, v_out, done.at[1]),
        pltpu.make_async_copy(pre_in, pre_out, done.at[2]),
        pltpu.make_async_copy(dec_in, dec_out, done.at[3]),
    ]
    for copy in copies:
        copy.start()
    lane = lax.broadcasted_iota(jnp.int32, (1, n * cap), 1)
    row = meta_in[0, IDS : IDS + 1, :]
    for s in range(1, n):
        row = jnp.where(lane // cap == s, meta_in[s, IDS : IDS + 1, :], row)
    ids[...] = row
    last = pltpu.make_async_copy(ids, ids_out, done.at[4])
    last.start()
    for copy in copies + [last]:
        copy.wait()


def write(n, cap, store_k, store_v, pre, dec, meta):
    vmem = pl.BlockSpec(memory_space=pltpu.VMEM)
    hbm = pl.BlockSpec(memory_space=pltpu.HBM)
    return pl.pallas_call(
        functools.partial(write_kernel, n, cap),
        in_specs=[vmem] * 5,
        out_specs=[hbm] * 5,
        out_shape=[jax.ShapeDtypeStruct(x.shape, x.dtype) for x in (store_k, store_v, pre, dec)]
        + [jax.ShapeDtypeStruct((1, n * cap), jnp.int32)],
        scratch_shapes=[pltpu.VMEM((1, n * cap), jnp.int32), pltpu.SemaphoreType.DMA((5,))],
        compiler_params=pltpu.CompilerParams(vmem_limit_bytes=16 << 20),
        name="write",
    )(store_k, store_v, pre, dec, meta)


def per_device(
    prefill_q, cache_k, cache_v, page_counts, page_owner, decode_q, decode_k, decode_v, context_len
):
    n = lax.axis_size("seq")
    groups = lax.axis_size("groups")
    page_slots = cache_k.shape[0] // PAGE
    cap = max(2, 2 * page_slots // n)
    split, _, _ = plan(n, cap)
    ck = cache_k.reshape(page_slots, PAGE, KVD)
    cv = cache_v.reshape(page_slots, PAGE, KVD)
    owner = page_owner[:, 0]
    parts = (page_counts, context_len, ck, cv, prefill_q, decode_q[0])
    pk, pv, *cross, q, meta = prep(n, cap, split, owner, *parts)
    pre, dec, store_k, store_v, meta, *flag = main(
        n, cap, split, groups, page_counts, q, meta, cache_k, cache_v, pk, pv,
        decode_k[0], decode_v[0], cross,
    )

    def keep(sk, sv, pre, dec, meta):
        return write(n, cap, sk, sv, pre, dec, meta)

    def again(sk, sv, pre, dec, meta):
        pk, pv, _, _ = prep(n, cap, False, owner, *parts)
        sk, sv = direct(n, cap, pk, pv)
        return write(n, cap, sk, sv, pre, dec, meta)

    if split:
        results = lax.cond(flag[0][0] > 0, again, keep, store_k, store_v, pre, dec, meta)
    else:
        results = keep(store_k, store_v, pre, dec, meta)
    store_k, store_v, pre, dec, ids = results
    return (
        pre,
        dec.reshape(1, STEPS, HQ * HD),
        store_k.reshape(-1, KVD),
        store_v.reshape(-1, KVD),
        ids.reshape(-1),
    )


def solution(mesh):
    both = ("groups", "seq")
    in_specs = (
        P(both, None),
        P(both, None),
        P(both, None),
        P("groups"),
        P(both, None),
        P(both, None, None),
        P(both, None, None),
        P(both, None, None),
        P(both),
    )
    out_specs = (
        P(both, None),
        P(both, None, None),
        P(both, None),
        P(both, None),
        P(both),
    )
    return jax.shard_map(
        per_device, mesh=mesh, in_specs=in_specs, out_specs=out_specs, check_vma=False
    )
```
